32 devices in a mesh: groups: 2 (over y), seq: 4 (over z), head: 2 (over x), loader: 2 (over core).
Axes of the slice: x: 2, y: 2, z: 4, core: 2. Of those that a mesh axis runs over, the one named last changes fastest.
Arguments:
- queries: bfloat16 [20480, 512], P(('groups', 'seq', 'loader'), 'head'), parts along dimension 0, may hold values from -6 to 6
- key_rows: bfloat16 [20480, 512], P(('groups', 'seq', 'loader'), 'head'), parts along dimension 0, may hold values from -6 to 6
- values: bfloat16 [20480, 512], P(('groups', 'seq', 'loader'), 'head'), parts along dimension 0, may hold values from -6 to 6
- cotangent: bfloat16 [20480, 512], P(('groups', 'seq', 'loader'), 'head'), parts along dimension 0, may hold values from -6 to 6
- out_gain: float32 [512], P('head'), may hold values from 0.1 to 1.9
- counts: int32 [16], P(('groups', 'seq', 'loader')), parts along dimension 0, may hold values from 1 to 5, as said below
Outputs:
- grad_query: bfloat16 [20480, 512], P(('groups', 'seq', 'loader'), 'head'), parts along dimension 0
- grad_key: bfloat16 [20480, 512], P(('groups', 'seq', 'loader'), 'head'), parts along dimension 0
- grad_value: bfloat16 [20480, 512], P(('groups', 'seq', 'loader'), 'head'), parts along dimension 0
The draws below stay inside these ranges and needn't reach their ends.
There are 2 independent parts, one for each index of `groups`. The reference program is written for one: setup_inputs(seed, part) draws one part's arguments, and reference() takes and returns one part's arrays. A program takes and returns all parts, laid end to end along the dimension named above; an argument that names none is the same for every part. Nothing has to cross between parts.
Inputs may be any that keep to these rules, and one draw needn't show every extreme that they name: `counts`: for each seq index the buffers of its two loader indices hold 6 live blocks together.
All inputs are finite; a program needn't handle non-finite values.
Results may differ from the reference program's by a relative error of at most 0.0059.
Values may be sent and summed in bfloat16 or wider, within the bound.
No kernel may reach another device: no remote copies, remote signals or barrier semaphores. Data moves between devices by JAX's collectives and lax.ppermute only.
A program may use at most 64 MiB of HBM per device.

```python
import jax
import jax.numpy as jnp
from jax import lax

DH = 128
SPAN = 256
HALF = 3
BUF = 5
CHAIN = 8
SLOTS = 10240
HEADS = 4
WIDTH = 512


def draw_counts(key, part):
    pair_count = CHAIN // 2
    key_split = jax.random.fold_in(key, 11)
    key_full = jax.random.fold_in(key, 23)
    key_side = jax.random.fold_in(key, 37)
    lower_blocks = jax.random.randint(key_split, (pair_count,), 1, 2 * HALF, dtype=jnp.int32)
    fullest = jax.random.randint(key_full, (), 0, pair_count, dtype=jnp.int32)
    side_bit = jax.random.randint(key_side, (), 0, 2, dtype=jnp.int32)
    forced = jnp.where(side_bit == 0, 2 * HALF - 1, 1).astype(jnp.int32)
    lower_blocks = jnp.where(jnp.arange(pair_count, dtype=jnp.int32) == fullest, forced, lower_blocks)
    return jnp.stack([lower_blocks, 2 * HALF - lower_blocks], axis=1).reshape(CHAIN).astype(jnp.int32)


def level_of(key, shape, cuts, smallest, high):
    def one(axis_at, shards_of):
        steps = jax.random.uniform(jax.random.fold_in(jax.random.fold_in(key, 6), axis_at), (shards_of,), jnp.float32, smallest / len(cuts), high / len(cuts))
        return jnp.repeat(jnp.exp(steps), shape[axis_at] // shards_of).reshape((-1,) + (1,) * (len(shape) - axis_at - 1))

    loudness = one(*cuts[0])
    for cut in cuts[1:]:
        loudness = loudness * one(*cut)
    return loudness


def gaussian(key, extent, scale, bound, cuts=(), kind=jnp.bfloat16):
    values = scale * jax.random.normal(key, extent, jnp.float32)
    if cuts:
        values = values * level_of(key, extent, cuts, -0.22, 0.18)
    return jnp.clip(values, -bound, bound).astype(kind)


def setup_inputs(seed: int = 0, part: int = 0) -> dict:
    seeds = jax.random.split(jax.random.key(seed), 7)
    own_keys = jax.random.split(jax.random.fold_in(seeds[6], part), 7)
    queries = gaussian(own_keys[0], (SLOTS, WIDTH), 1.0, 6.0, ((0, 8), (1, 2)))
    key_rows = gaussian(own_keys[1], (SLOTS, WIDTH), 1.0, 6.0, ((0, 8), (1, 2)))
    values = gaussian(own_keys[2], (SLOTS, WIDTH), 1.0, 6.0, ((0, 8), (1, 2)))
    cotangent = gaussian(own_keys[3], (SLOTS, WIDTH), 1.0, 6.0, ((0, 8), (1, 2)))
    out_gain = jnp.clip(1.0 + 0.18 * jax.random.normal(seeds[4], (WIDTH,), jnp.float32), 0.1, 1.9)
    counts = draw_counts(jax.random.fold_in(jax.random.fold_in(seeds[6], part), 71), part)
    return dict(queries=queries, key_rows=key_rows, values=values, cotangent=cotangent, out_gain=out_gain, counts=counts)


epsilon = 1e-06

def exclusive_prefix(states):
    zero_state = jnp.zeros((1,) + states.shape[1:], jnp.float32)
    return jnp.concatenate([zero_state, jnp.cumsum(states[:-1], axis=0)], axis=0)

def exclusive_suffix(states):
    zero_state = jnp.zeros((1,) + states.shape[1:], jnp.float32)
    later_sum = jnp.flip(jnp.cumsum(jnp.flip(states[1:], 0), axis=0), 0)
    return jnp.concatenate([later_sum, zero_state], axis=0)

def to_half(array):
    rounded = lax.optimization_barrier(array.astype(jnp.bfloat16))
    return rounded.astype(jnp.float32)

def one_head(pieces):
    queries, key_rows, values, cotangent, gain_row = pieces
    query_f = queries.astype(jnp.float32)
    key_f = key_rows.astype(jnp.float32)
    value_f = values.astype(jnp.float32)
    length = queries.shape[1]
    row_ids = lax.broadcasted_iota(jnp.int32, (length, length), 0)
    col_ids = lax.broadcasted_iota(jnp.int32, (length, length), 1)
    visible = (row_ids >= col_ids)[None]
    states = jnp.einsum('bcd,bce->bde', key_f, value_f)
    prefix_f = to_half(exclusive_prefix(states))
    scores = jnp.einsum('bcd,bsd->bcs', query_f, key_f)
    scored_f = to_half(jnp.where(visible, scores, jnp.zeros((), jnp.float32)))
    raw_out = jnp.einsum('bcd,bde->bce', query_f, prefix_f) + jnp.einsum('bcs,bse->bce', scored_f, value_f)
    inverse_rms = lax.rsqrt(lax.optimization_barrier(jnp.mean(raw_out * raw_out, axis=-1, keepdims=True)) + epsilon)
    weighted = gain_row * cotangent.astype(jnp.float32)
    grad_raw = inverse_rms * weighted - raw_out * inverse_rms ** 3 * lax.optimization_barrier(jnp.mean(weighted * raw_out, axis=-1, keepdims=True))
    grad_f = to_half(grad_raw)
    back_states = jnp.einsum('bcd,bce->bde', query_f, grad_f)
    suffix_f = to_half(exclusive_suffix(back_states))
    pulled = jnp.einsum('bce,bse->bcs', grad_f, value_f)
    pull_f = to_half(jnp.where(visible, pulled, jnp.zeros((), jnp.float32)))
    grad_query = jnp.einsum('bce,bde->bcd', grad_f, prefix_f) + jnp.einsum('bcs,bsd->bcd', pull_f, key_f)
    grad_key = jnp.einsum('bse,bde->bsd', value_f, suffix_f) + jnp.einsum('bcs,bcd->bsd', pull_f, query_f)
    grad_value = jnp.einsum('bsd,bde->bse', key_f, suffix_f) + jnp.einsum('bcs,bce->bse', scored_f, grad_f)
    return (grad_query.astype(jnp.bfloat16), grad_key.astype(jnp.bfloat16), grad_value.astype(jnp.bfloat16))

def reference(queries, key_rows, values, cotangent, out_gain, counts):
    block_total = CHAIN * BUF
    block_ids = jnp.arange(block_total, dtype=jnp.int32)
    owners = (block_ids // BUF).astype(jnp.int32)
    live_mask = block_ids % BUF < counts[owners]

    def per_head(array):
        shaped = array.reshape(block_total, SPAN, HEADS, DH)
        shaped = jnp.where(live_mask[:, None, None, None], shaped, jnp.zeros((), array.dtype))
        return jnp.moveaxis(shaped, 2, 0)
    gain_rows = out_gain.reshape(HEADS, 1, 1, DH)
    grad_query, grad_key, grad_value = lax.map(one_head, (per_head(queries), per_head(key_rows), per_head(values), per_head(cotangent), gain_rows))
    grad_query = jnp.moveaxis(grad_query, 0, 2).reshape(SLOTS, WIDTH)
    grad_key = jnp.moveaxis(grad_key, 0, 2).reshape(SLOTS, WIDTH)
    grad_value = jnp.moveaxis(grad_value, 0, 2).reshape(SLOTS, WIDTH)
    return (grad_query, grad_key, grad_value)
```

```python
import functools

import jax
import jax.numpy as jnp
from jax import lax
from jax.experimental import pallas as pl
from jax.experimental.pallas import tpu as pltpu
from jax.sharding import PartitionSpec as P

DH = 128
SPAN = 256
EPSILON = 1e-06
F32 = jnp.float32
BF16 = jnp.bfloat16
VMEM = pl.BlockSpec(memory_space=pltpu.VMEM)
SMEM = pl.BlockSpec(memory_space=pltpu.SMEM)


def nn(a, b):
    return lax.dot_general(a, b, (((1,), (0,)), ((), ())), preferred_element_type=F32)


def nt(a, b):
    return lax.dot_general(a, b, (((1,), (1,)), ((), ())), preferred_element_type=F32)


def tn(a, b):
    return lax.dot_general(a, b, (((0,), (0,)), ((), ())), preferred_element_type=F32)


def tiles(rows, width):
    for b in range(rows // SPAN):
        for h in range(width // DH):
            yield b, h, slice(b * SPAN, (b + 1) * SPAN), slice(h * DH, (h + 1) * DH)


def state_kernel(count_ref, k_ref, v_ref, run_ref, total_ref):
    running = {}
    for b, h, r, c in tiles(*k_ref.shape):
        state = tn(k_ref[r, c], v_ref[r, c])
        state = jnp.where(b < count_ref[0], state, jnp.zeros_like(state))
        if b == 0:
            run_ref[b, h] = jnp.zeros_like(state)
            running[h] = state
        else:
            run_ref[b, h] = running[h]
            running[h] = running[h] + state
    for h, state in running.items():
        total_ref[h] = state.astype(total_ref.dtype)


def score_kernel(q_ref, k_ref, v_ref, part_ref, turned_ref):
    t = lax.broadcasted_iota(jnp.int32, (SPAN, SPAN), 0)
    s = lax.broadcasted_iota(jnp.int32, (SPAN, SPAN), 1)
    for b, h, r, c in tiles(*q_ref.shape):
        q, k = q_ref[r, c], k_ref[r, c]
        scored = jnp.where(t >= s, nt(q, k), 0.0).astype(BF16)
        part_ref[r, c] = nn(scored, v_ref[r, c])
        turned_ref[b, h] = jnp.where(t <= s, nt(k, q), 0.0).astype(BF16)


def norm_kernel(count_ref, q_ref, cot_ref, gain_ref, part_ref, run_ref, near_ref, far_ref,
                grad_ref, prefix_ref, back_ref, total_ref):
    running = {}
    for b, h, r, c in reversed(list(tiles(*q_ref.shape))):
        prefix = (run_ref[b, h] + near_ref[h] + far_ref[h]).astype(BF16)
        prefix_ref[b, h] = prefix
        q = q_ref[r, c]
        raw = part_ref[r, c] + nn(q, prefix)
        inverse = lax.rsqrt(jnp.mean(raw * raw, axis=-1, keepdims=True) + EPSILON)
        gain = gain_ref[:, c]
        gain = jnp.where(b < count_ref[0], gain, jnp.zeros_like(gain))
        weighted = gain * cot_ref[r, c].astype(F32)
        pulled = jnp.mean(weighted * raw, axis=-1, keepdims=True)
        grad = (inverse * weighted - raw * (inverse * inverse * inverse * pulled)).astype(BF16)
        grad_ref[r, c] = grad
        state = tn(q, grad)
        back_ref[b, h] = running.get(h, jnp.zeros_like(state))
        running[h] = running[h] + state if h in running else state
    for h, state in running.items():
        total_ref[h] = state.astype(total_ref.dtype)


def pull_kernel(q_ref, k_ref, v_ref, grad_ref, turned_ref, prefix_ref, gq_ref, gk_ref, gv_ref):
    t = lax.broadcasted_iota(jnp.int32, (SPAN, SPAN), 0)
    s = lax.broadcasted_iota(jnp.int32, (SPAN, SPAN), 1)
    for b, h, r, c in tiles(*q_ref.shape):
        v, grad = v_ref[r, c], grad_ref[r, c]
        pull = jnp.where(t >= s, nt(grad, v), 0.0).astype(BF16)
        gq_ref[r, c] = (nn(pull, k_ref[r, c]) + nt(grad, prefix_ref[b, h])).astype(BF16)
        turned = jnp.where(t <= s, nt(v, grad), 0.0).astype(BF16)
        gk_ref[r, c] = nn(turned, q_ref[r, c])
        gv_ref[r, c] = nn(turned_ref[b, h], grad)


def final_kernel(count_ref, k_ref, v_ref, gk_part_ref, gv_part_ref, back_ref, near_ref, far_ref,
                 gk_ref, gv_ref):
    for b, h, r, c in tiles(*k_ref.shape):
        suffix = back_ref[b, h] + near_ref[h] + far_ref[h]
        suffix = jnp.where(b < count_ref[0], suffix, jnp.zeros_like(suffix)).astype(BF16)
        gk_ref[r, c] = (gk_part_ref[r, c] + nt(v_ref[r, c], suffix)).astype(BF16)
        gv_ref[r, c] = (gv_part_ref[r, c] + nn(k_ref[r, c], suffix)).astype(BF16)


def call(kernel, out_shape, flops, *args):
    specs = [SMEM if a.dtype == jnp.int32 else VMEM for a in args]
    size = sum(a.size * a.dtype.itemsize for a in args)
    size += sum(a.size * a.dtype.itemsize for a in out_shape)
    return pl.pallas_call(
        kernel,
        out_shape=out_shape,
        in_specs=specs,
        out_specs=[VMEM] * len(out_shape),
        cost_estimate=pl.CostEstimate(flops=flops, bytes_accessed=size, transcendentals=0),
        compiler_params=pltpu.CompilerParams(vmem_limit_bytes=32 * 2**20),
    )(*args)


def radices(count):
    found = []
    for radix in (4, 2):
        while count % radix == 0:
            found.append(radix)
            count //= radix
    return found + [count] if count > 1 else found


def chip_sums(total, reverse):
    count, place = lax.axis_size("seq"), lax.axis_index("seq")
    outside = jnp.zeros(total.shape, F32)
    group, stride = total, 1
    chain = radices(count)
    for at, radix in enumerate(chain):
        digit = place // stride % radix
        whole = group.astype(F32)
        for step in range(1, radix):
            def partner(d, step=step):
                return d ^ step if radix in (2, 4) else (d + step) % radix
            pairs = [(s, s + (partner(s // stride % radix) - s // stride % radix) * stride)
                     for s in range(count)]
            came = lax.ppermute(group, "seq", pairs).astype(F32)
            source = digit ^ step if radix in (2, 4) else (digit + radix - step) % radix
            use = source > digit if reverse else source < digit
            outside = outside + jnp.where(use, came, 0.0)
            whole = whole + came
        if at + 1 < len(chain):
            group = whole.astype(total.dtype)
        stride *= radix
    return outside


def outside_sum(total, reverse):
    near = chip_sums(total, reverse)
    core = lax.axis_index("loader")
    mine = core == (1 if reverse else 0)
    sent = near + jnp.where(mine, total.astype(F32), 0.0)
    far = lax.ppermute(sent, "loader", [(0, 1), (1, 0)])
    return near, far


def shards(queries, key_rows, values, cotangent, out_gain, counts):
    rows, width = queries.shape
    blocks, heads = rows // SPAN, width // DH
    unit = 2 * rows * width * DH
    like = jax.ShapeDtypeStruct
    states = like((blocks, heads, DH, DH), F32)
    total = like((heads, DH, DH), BF16)
    plane = like((rows, width), F32)
    half = like((rows, width), BF16)
    square = like((blocks, heads, SPAN, SPAN), BF16)
    gain_row = out_gain.reshape(1, width)

    run, own = call(state_kernel, [states, total], unit, counts, key_rows, values)
    near, far = outside_sum(own, False)
    part, turned = call(score_kernel, [plane, square], 6 * unit, queries, key_rows, values)
    grad, prefix, back, own_back = call(
        norm_kernel, [half, like(states.shape, BF16), states, total], 2 * unit,
        counts, queries, cotangent, gain_row, part, run, near, far)
    near, far = outside_sum(own_back, True)
    gq, gk_part, gv_part = call(
        pull_kernel, [half, plane, plane], 11 * unit,
        queries, key_rows, values, grad, turned, prefix)
    gk, gv = call(final_kernel, [half, half], 2 * unit,
                  counts, key_rows, values, gk_part, gv_part, back, near, far)
    return gq, gk, gv


def solution(mesh):
    rows = P(("groups", "seq", "loader"), "head")
    return jax.shard_map(
        shards,
        mesh=mesh,
        in_specs=(rows, rows, rows, rows, P("head"), P(("groups", "seq", "loader"))),
        out_specs=(rows, rows, rows),
        check_vma=False,
    )
```

```python
import functools
import math

import jax
import jax.numpy as jnp
from jax import lax
from jax.experimental import pallas as pl
from jax.experimental.pallas import tpu as pltpu
from jax.sharding import PartitionSpec as P

DH = 128
SPAN = 256
EPSILON = 1e-06
F32 = jnp.float32
BF16 = jnp.bfloat16
VMEM = pl.BlockSpec(memory_space=pltpu.VMEM)
SMEM = pl.BlockSpec(memory_space=pltpu.SMEM)
HBM = pl.BlockSpec(memory_space=pltpu.HBM)


def nn(a, b):
    return lax.dot_general(a, b, (((1,), (0,)), ((), ())), preferred_element_type=F32)


def nt(a, b):
    return lax.dot_general(a, b, (((1,), (1,)), ((), ())), preferred_element_type=F32)


def tn(a, b):
    return lax.dot_general(a, b, (((0,), (0,)), ((), ())), preferred_element_type=F32)


def tiles(rows, width):
    for b in range(rows // SPAN):
        for h in range(width // DH):
            yield b, h, slice(b * SPAN, (b + 1) * SPAN), slice(h * DH, (h + 1) * DH)


def fetch(pairs, sems):
    copies = []
    for b in range(pairs[0][0].shape[0] // SPAN):
        r = pl.ds(b * SPAN, SPAN)
        copies.append([pltpu.make_async_copy(source.at[r], target.at[r], sems.at[b, at])
                       for at, (source, target) in enumerate(pairs)])
        for copy in copies[-1]:
            copy.start()
    return copies


def wait(copies):
    for copy in copies:
        copy.wait()


def state_of(count_ref, b, k, v):
    state = tn(k, v)
    return jnp.where(b < count_ref[0], state, jnp.zeros_like(state))


def state_kernel(count_ref, k_hbm, v_hbm, total_ref, k_ref, v_ref, sems):
    copies = fetch(((k_hbm, k_ref), (v_hbm, v_ref)), sems)
    running = {}
    for b, h, r, c in tiles(*k_ref.shape):
        if h == 0:
            wait(copies[b])
        state = state_of(count_ref, b, k_ref[r, c], v_ref[r, c])
        running[h] = running[h] + state if b else state
    for h, state in running.items():
        total_ref[h] = state.astype(total_ref.dtype)


def score_kernel(count_ref, q_hbm, cot_hbm, k_ref, v_ref,
                 part_ref, turned_ref, run_ref, q_ref, cot_ref, sems):
    copies = fetch(((q_hbm, q_ref), (cot_hbm, cot_ref)), sems)
    running = {}
    t = lax.broadcasted_iota(jnp.int32, (SPAN, SPAN), 0)
    s = lax.broadcasted_iota(jnp.int32, (SPAN, SPAN), 1)
    for b, h, r, c in tiles(*q_ref.shape):
        if h == 0:
            wait(copies[b])
        q, k, v = q_ref[r, c], k_ref[r, c], v_ref[r, c]
        state = state_of(count_ref, b, k, v)
        run_ref[b, h] = running[h] if b else jnp.zeros_like(state)
        running[h] = running[h] + state if b else state
        scored = jnp.where(t >= s, nt(q, k), 0.0).astype(BF16)
        part_ref[r, c] = nn(scored, v)
        turned_ref[b, h] = jnp.where(t <= s, nt(k, q), 0.0).astype(BF16)


def norm_kernel(count_ref, q_ref, cot_ref, gain_ref, part_ref, run_ref, near_ref, far_ref,
                grad_ref, prefix_ref, back_ref, total_ref):
    running = {}
    for b, h, r, c in reversed(list(tiles(*q_ref.shape))):
        prefix = (run_ref[b, h] + near_ref[h] + far_ref[h]).astype(BF16)
        prefix_ref[b, h] = prefix
        q = q_ref[r, c]
        raw = part_ref[r, c] + nn(q, prefix)
        inverse = lax.rsqrt(jnp.mean(raw * raw, axis=-1, keepdims=True) + EPSILON)
        gain = gain_ref[:, c]
        gain = jnp.where(b < count_ref[0], gain, jnp.zeros_like(gain))
        weighted = gain * cot_ref[r, c].astype(F32)
        pulled = jnp.mean(weighted * raw, axis=-1, keepdims=True)
        grad = (inverse * weighted - raw * (inverse * inverse * inverse * pulled)).astype(BF16)
        grad_ref[r, c] = grad
        state = tn(q, grad)
        back_ref[b, h] = running.get(h, jnp.zeros_like(state))
        running[h] = running[h] + state if h in running else state
    for h, state in running.items():
        total_ref[h] = state.astype(total_ref.dtype)


def pull_kernel(q_ref, k_ref, v_ref, grad_ref, turned_ref, prefix_ref,
                gq_hbm, gk_ref, gv_ref, gq_ref, sems):
    t = lax.broadcasted_iota(jnp.int32, (SPAN, SPAN), 0)
    s = lax.broadcasted_iota(jnp.int32, (SPAN, SPAN), 1)
    heads = q_ref.shape[1] // DH
    copies = []
    for b, h, r, c in tiles(*q_ref.shape):
        v, grad = v_ref[r, c], grad_ref[r, c]
        pull = jnp.where(t >= s, nt(grad, v), 0.0).astype(BF16)
        gq_ref[r, c] = (nn(pull, k_ref[r, c]) + nt(grad, prefix_ref[b, h])).astype(BF16)
        if h == heads - 1:
            copies.append(pltpu.make_async_copy(gq_ref.at[r], gq_hbm.at[r], sems.at[b]))
            copies[-1].start()
        turned = jnp.where(t <= s, nt(v, grad), 0.0).astype(BF16)
        gk_ref[r, c] = nn(turned, q_ref[r, c])
        gv_ref[r, c] = nn(turned_ref[b, h], grad)
    wait(copies)


def final_kernel(count_ref, k_ref, v_ref, gk_part_ref, gv_part_ref, back_ref, near_ref, far_ref,
                 gk_hbm, gv_hbm, gk_ref, gv_ref, sems):
    heads = k_ref.shape[1] // DH
    copies = []
    for b, h, r, c in tiles(*k_ref.shape):
        suffix = back_ref[b, h] + near_ref[h] + far_ref[h]
        suffix = jnp.where(b < count_ref[0], suffix, jnp.zeros_like(suffix)).astype(BF16)
        gk_ref[r, c] = (gk_part_ref[r, c] + nt(v_ref[r, c], suffix)).astype(BF16)
        gv_ref[r, c] = (gv_part_ref[r, c] + nn(k_ref[r, c], suffix)).astype(BF16)
        if h == heads - 1:
            for at, (source, target) in enumerate(((gk_ref, gk_hbm), (gv_ref, gv_hbm))):
                copies.append(pltpu.make_async_copy(source.at[r], target.at[r], sems.at[b, at]))
                copies[-1].start()
    wait(copies)


def place(array, space):
    return array if space is SMEM else pltpu.with_memory_space_constraint(array, space.memory_space)


def call(kernel, ins, outs, flops, scratch=()):
    size = sum(a.size * a.dtype.itemsize for a, _ in ins)
    size += sum(math.prod(shape) * jnp.dtype(kind).itemsize for (shape, kind), _ in outs)
    return pl.pallas_call(
        kernel,
        out_shape=[pltpu.VMEM(*a) if space is VMEM else pltpu.HBM(*a) for a, space in outs],
        in_specs=[space for _, space in ins],
        out_specs=[space for _, space in outs],
        scratch_shapes=scratch,
        cost_estimate=pl.CostEstimate(flops=flops, bytes_accessed=size, transcendentals=0),
        compiler_params=pltpu.CompilerParams(vmem_limit_bytes=16 * 2**20),
    )(*[place(a, space) for a, space in ins])


def radices(count):
    found = []
    for radix in (4, 2):
        while count % radix == 0:
            found.append(radix)
            count //= radix
    return found + [count] if count > 1 else found


def partner(digit, step, radix):
    return digit ^ step if radix in (2, 4) else (digit + step) % radix


def combine_kernel(steps, radix, stride, reverse, last, *refs):
    own_ref, group_ref, outside_ref = refs[:3]
    came = refs[3:3 + len(steps)]
    near_ref, sent_ref = refs[3 + len(steps):]
    digit = lax.rem(lax.div(lax.axis_index("seq"), stride), radix)
    near = outside_ref[...]
    whole = group_ref[...].astype(F32)
    for step, piece_ref in zip(steps, came):
        back = step if radix in (2, 4) else radix - step
        source = partner(digit, back, radix)
        use = source > digit if reverse else source < digit
        piece = piece_ref[...].astype(F32)
        near = near + jnp.where(use, piece, 0.0)
        whole = whole + piece
    near_ref[...] = near
    if last:
        mine = lax.axis_index("loader") == (1 if reverse else 0)
        sent_ref[...] = near + jnp.where(mine, own_ref[...].astype(F32), 0.0)
    else:
        sent_ref[...] = whole.astype(sent_ref.dtype)


def outside_sum(total, reverse, cover):
    count = lax.axis_size("seq")
    outside = jnp.zeros(total.shape, F32)
    group, stride = total, 1
    chain = radices(count)
    for at, radix in enumerate(chain):
        steps = list(range(radix - 1, 0, -1))
        came = []
        for step in steps:
            pairs = [(s, s + (partner(s // stride % radix, step, radix) - s // stride % radix) * stride)
                     for s in range(count)]
            came.append(lax.ppermute(group, "seq", pairs))
        if at == 0:
            came, cover = lax.optimization_barrier((came, cover))
        last = at + 1 == len(chain)
        kernel = functools.partial(combine_kernel, steps, radix, stride, reverse, last)
        sum_like = (total.shape, F32), VMEM
        outside, group = call(
            kernel, [(a, VMEM) for a in (total, group, outside, *came)],
            [sum_like, sum_like if last else ((total.shape, total.dtype), VMEM)], total.size)
        stride *= radix
    far = lax.ppermute(group, "loader", [(0, 1), (1, 0)])
    return outside, far, cover


def shards(queries, key_rows, values, cotangent, out_gain, counts):
    rows, width = queries.shape
    blocks, heads = rows // SPAN, width // DH
    unit = 2 * rows * width * DH
    states = ((blocks, heads, DH, DH), F32), VMEM
    prefixes = ((blocks, heads, DH, DH), BF16), VMEM
    total = ((heads, DH, DH), BF16), VMEM
    plane = ((rows, width), F32), VMEM
    half = ((rows, width), BF16), VMEM
    result = ((rows, width), BF16), HBM
    square = ((blocks, heads, SPAN, SPAN), BF16), VMEM
    staged = pltpu.VMEM((rows, width), BF16)
    pair_sems = pltpu.SemaphoreType.DMA((blocks, 2))

    def vmem(*arrays):
        return [(a, VMEM) for a in arrays]

    count = [(counts, SMEM)]
    own, k, v = call(
        state_kernel, count + [(key_rows, HBM), (values, HBM)], [total, half, half], unit, [pair_sems])
    cover = call(
        score_kernel, count + [(queries, HBM), (cotangent, HBM)] + vmem(k, v),
        [plane, square, states, half, half], 7 * unit, [pair_sems])
    near, far, (part, turned, run, q, cot) = outside_sum(own, False, cover)
    grad, prefix, back, own_back = call(
        norm_kernel, count + vmem(q, cot, out_gain.reshape(1, width), part, run, near, far),
        [half, prefixes, states, total], 2 * unit)
    cover = call(
        pull_kernel, vmem(q, k, v, grad, turned, prefix), [result, plane, plane], 11 * unit,
        [staged, pltpu.SemaphoreType.DMA((blocks,))])
    near, far, (gq, gk_part, gv_part) = outside_sum(own_back, True, cover)
    gk, gv = call(
        final_kernel, count + vmem(k, v, gk_part, gv_part, back, near, far), [result, result], 2 * unit,
        [staged, staged, pair_sems])
    return gq, gk, gv


def solution(mesh):
    rows = P(("groups", "seq", "loader"), "head")
    return jax.shard_map(
        shards,
        mesh=mesh,
        in_specs=(rows, rows, rows, rows, P("head"), P(("groups", "seq", "loader"))),
        out_specs=(rows, rows, rows),
        check_vma=False,
    )
```

```python
import functools
import math

import jax
import jax.numpy as jnp
from jax import lax
from jax.experimental import pallas as pl
from jax.experimental.pallas import tpu as pltpu
from jax.sharding import PartitionSpec as P

DH = 128
SPAN = 256
EPSILON = 1e-06
F32 = jnp.float32
BF16 = jnp.bfloat16
VMEM = pl.BlockSpec(memory_space=pltpu.VMEM)
SMEM = pl.BlockSpec(memory_space=pltpu.SMEM)
HBM = pl.BlockSpec(memory_space=pltpu.HBM)


def nn(a, b):
    return lax.dot_general(a, b, (((1,), (0,)), ((), ())), preferred_element_type=F32)


def nt(a, b):
    return lax.dot_general(a, b, (((1,), (1,)), ((), ())), preferred_element_type=F32)


def tn(a, b):
    return lax.dot_general(a, b, (((0,), (0,)), ((), ())), preferred_element_type=F32)


def tiles(rows, width):
    for b in range(rows // SPAN):
        for h in range(width // DH):
            yield b, h, slice(b * SPAN, (b + 1) * SPAN), slice(h * DH, (h + 1) * DH)


def fetch(pairs, sems):
    copies = [pltpu.make_async_copy(source, target, sems.at[at]) for at, (source, target) in enumerate(pairs)]
    for copy in copies:
        copy.start()
    return copies


def wait(copies):
    for copy in copies:
        copy.wait()


def state_of(count_ref, b, k, v):
    state = tn(k, v)
    return jnp.where(b < count_ref[0], state, jnp.zeros_like(state))


def halves(total, h, keep_ref, give_ref):
    first = lax.axis_index("loader") == 0
    low, high = total[:DH // 2], total[DH // 2:]
    keep_ref[h] = jnp.where(first, low, high)
    give_ref[h] = jnp.where(first, high, low).astype(give_ref.dtype)


def state_kernel(count_ref, k_hbm, v_hbm, q_hbm, keep_ref, give_ref, k_ref, v_ref, q_ref, sems):
    copies = fetch(((k_hbm, k_ref), (v_hbm, v_ref), (q_hbm, q_ref)), sems)
    wait(copies[:2])
    running = {}
    for b, h, r, c in tiles(*k_ref.shape):
        state = state_of(count_ref, b, k_ref[r, c], v_ref[r, c])
        running[h] = running[h] + state if b else state
    for h, state in running.items():
        halves(state, h, keep_ref, give_ref)
    wait(copies[2:])


def score_kernel(count_ref, cot_hbm, q_ref, k_ref, v_ref, part_ref, turned_ref, run_ref, cot_ref, sems):
    copies = fetch(((cot_hbm, cot_ref),), sems)
    running = {}
    t = lax.broadcasted_iota(jnp.int32, (SPAN, SPAN), 0)
    s = lax.broadcasted_iota(jnp.int32, (SPAN, SPAN), 1)
    for b, h, r, c in tiles(*q_ref.shape):
        q, k, v = q_ref[r, c], k_ref[r, c], v_ref[r, c]
        state = state_of(count_ref, b, k, v)
        run_ref[b, h] = running[h] if b else jnp.zeros_like(state)
        running[h] = running[h] + state if b else state
        scored = jnp.where(t >= s, nt(q, k), 0.0).astype(BF16)
        part_ref[r, c] = nn(scored, v)
        turned_ref[b, h] = jnp.where(t <= s, nt(k, q), 0.0).astype(BF16)
    wait(copies)


def joined(near_ref, far_ref):
    first = lax.axis_index("loader") == 0
    sums = []
    for h in range(near_ref.shape[0]):
        near, far = near_ref[h], far_ref[h]
        sums.append(jnp.concatenate([jnp.where(first, near, far), jnp.where(first, far, near)], axis=0))
    return sums


def norm_kernel(count_ref, q_ref, cot_ref, gain_ref, part_ref, run_ref, near_ref, far_ref,
                grad_ref, prefix_ref, back_ref, keep_ref, give_ref):
    running = {}
    outside = joined(near_ref, far_ref)
    for b, h, r, c in reversed(list(tiles(*q_ref.shape))):
        prefix = (run_ref[b, h] + outside[h]).astype(BF16)
        prefix_ref[b, h] = prefix
        q = q_ref[r, c]
        raw = part_ref[r, c] + nn(q, prefix)
        inverse = lax.rsqrt(jnp.mean(raw * raw, axis=-1, keepdims=True) + EPSILON)
        gain = gain_ref[:, c]
        gain = jnp.where(b < count_ref[0], gain, jnp.zeros_like(gain))
        weighted = gain * cot_ref[r, c].astype(F32)
        pulled = jnp.mean(weighted * raw, axis=-1, keepdims=True)
        grad = (inverse * weighted - raw * (inverse * inverse * inverse * pulled)).astype(BF16)
        grad_ref[r, c] = grad
        state = tn(q, grad)
        back_ref[b, h] = running.get(h, jnp.zeros_like(state))
        running[h] = running[h] + state if h in running else state
    for h, state in running.items():
        halves(state, h, keep_ref, give_ref)


def value_kernel(grad_ref, turned_ref, gv_ref):
    for b, h, r, c in tiles(*grad_ref.shape):
        gv_ref[r, c] = nn(turned_ref[b, h], grad_ref[r, c])


def pull_kernel(q_ref, k_ref, v_ref, grad_ref, prefix_ref, gq_hbm, gk_ref, gq_ref, sems):
    t = lax.broadcasted_iota(jnp.int32, (SPAN, SPAN), 0)
    s = lax.broadcasted_iota(jnp.int32, (SPAN, SPAN), 1)
    for b, h, r, c in tiles(*q_ref.shape):
        v, grad = v_ref[r, c], grad_ref[r, c]
        pull = jnp.where(t >= s, nt(grad, v), 0.0).astype(BF16)
        gq_ref[r, c] = (nn(pull, k_ref[r, c]) + nt(grad, prefix_ref[b, h])).astype(BF16)
    copies = fetch(((gq_ref, gq_hbm),), sems)
    for b, h, r, c in tiles(*q_ref.shape):
        v, grad = v_ref[r, c], grad_ref[r, c]
        turned = jnp.where(t <= s, nt(v, grad), 0.0).astype(BF16)
        gk_ref[r, c] = nn(turned, q_ref[r, c])
    wait(copies)


def final_kernel(count_ref, k_ref, v_ref, gk_part_ref, gv_part_ref, back_ref, near_ref, far_ref,
                 gk_hbm, gv_hbm, gk_ref, gv_ref, sems):
    heads = k_ref.shape[1] // DH
    outside = joined(near_ref, far_ref)
    copies = []
    for b, h, r, c in tiles(*k_ref.shape):
        suffix = back_ref[b, h] + outside[h]
        suffix = jnp.where(b < count_ref[0], suffix, jnp.zeros_like(suffix)).astype(BF16)
        gk_ref[r, c] = (gk_part_ref[r, c] + nt(v_ref[r, c], suffix)).astype(BF16)
        gv_ref[r, c] = (gv_part_ref[r, c] + nn(k_ref[r, c], suffix)).astype(BF16)
        if h == heads - 1:
            for at, (source, target) in enumerate(((gk_ref, gk_hbm), (gv_ref, gv_hbm))):
                copies.append(pltpu.make_async_copy(source.at[r], target.at[r], sems.at[b, at]))
                copies[-1].start()
    wait(copies)


def place(array, space):
    return array if space is SMEM else pltpu.with_memory_space_constraint(array, space.memory_space)


def call(kernel, ins, outs, flops, scratch=()):
    size = sum(a.size * a.dtype.itemsize for a, _ in ins)
    size += sum(math.prod(shape) * jnp.dtype(kind).itemsize for (shape, kind), _ in outs)
    return pl.pallas_call(
        kernel,
        out_shape=[pltpu.VMEM(*a) if space is VMEM else pltpu.HBM(*a) for a, space in outs],
        in_specs=[space for _, space in ins],
        out_specs=[space for _, space in outs],
        scratch_shapes=scratch,
        cost_estimate=pl.CostEstimate(flops=flops, bytes_accessed=size, transcendentals=0),
        compiler_params=pltpu.CompilerParams(vmem_limit_bytes=16 * 2**20),
    )(*[place(a, space) for a, space in ins])


def radices(count):
    found = []
    for radix in (4, 2):
        while count % radix == 0:
            found.append(radix)
            count //= radix
    return found + [count] if count > 1 else found


def partner(digit, step, radix):
    return digit ^ step if radix in (2, 4) else (digit + step) % radix


def pair_kernel(keep_ref, came_ref, group_ref):
    group_ref[...] = (keep_ref[...] + came_ref[...].astype(F32)).astype(group_ref.dtype)


def combine_kernel(steps, radix, stride, reverse, first, last, *refs):
    refs = list(refs)
    sent_ref, near_ref = refs.pop(), refs.pop()
    keep_ref, beside_ref, group_ref = refs[:3]
    came = refs[3:3 + len(steps)]
    digit = lax.rem(lax.div(lax.axis_index("seq"), stride), radix)
    near = jnp.zeros(near_ref.shape, F32) if first else refs[-1][...]
    whole = group_ref[...].astype(F32)
    for step, piece_ref in zip(steps, came):
        source = partner(digit, step if radix in (2, 4) else radix - step, radix)
        use = source > digit if reverse else source < digit
        piece = piece_ref[...].astype(F32)
        near = near + jnp.where(use, piece, 0.0)
        whole = whole + piece
    if last:
        ahead = lax.axis_index("loader") == (1 if reverse else 0)
        sent_ref[...] = near + jnp.where(ahead, keep_ref[...], 0.0)
        near_ref[...] = near + jnp.where(ahead, 0.0, beside_ref[...].astype(F32))
    else:
        near_ref[...] = near
        sent_ref[...] = whole.astype(sent_ref.dtype)


def order(radix, reverse):
    if radix == 4:
        return [1, 3, 2] if reverse else [1, 3, 2]
    return list(range(radix - 1, 0, -1))


def outside_sum(keep, give, reverse, core_cover, chip_cover):
    swap = [(0, 1), (1, 0)]
    beside, core_cover = lax.optimization_barrier((lax.ppermute(give, "loader", swap), core_cover))
    like = (keep.shape, F32), VMEM
    small = (keep.shape, give.dtype), VMEM
    group, = call(pair_kernel, [(keep, VMEM), (beside, VMEM)], [small], keep.size)
    count, stride, outside = lax.axis_size("seq"), 1, []
    chain = radices(count)
    for at, radix in enumerate(chain):
        steps = order(radix, reverse)
        came = []
        for step in steps:
            pairs = [(s, s + (partner(s // stride % radix, step, radix) - s // stride % radix) * stride)
                     for s in range(count)]
            came.append(lax.ppermute(group, "seq", pairs))
        if at == 0:
            came, chip_cover = lax.optimization_barrier((came, chip_cover))
        last = at + 1 == len(chain)
        kernel = functools.partial(combine_kernel, steps, radix, stride, reverse, at == 0, last)
        near, group = call(
            kernel, [(a, VMEM) for a in (keep, beside, group, *came, *outside)],
            [like, like if last else small], keep.size)
        outside = [near]
        stride *= radix
    far = lax.ppermute(group, "loader", swap)
    return near, far, core_cover, chip_cover


def shards(queries, key_rows, values, cotangent, out_gain, counts):
    rows, width = queries.shape
    blocks, heads = rows // SPAN, width // DH
    unit = 2 * rows * width * DH
    states = ((blocks, heads, DH, DH), F32), VMEM
    prefixes = ((blocks, heads, DH, DH), BF16), VMEM
    keep = ((heads, DH // 2, DH), F32), VMEM
    give = ((heads, DH // 2, DH), BF16), VMEM
    plane = ((rows, width), F32), VMEM
    half = ((rows, width), BF16), VMEM
    result = ((rows, width), BF16), HBM
    square = ((blocks, heads, SPAN, SPAN), BF16), VMEM
    staged = pltpu.VMEM((rows, width), BF16)
    pair_sems = pltpu.SemaphoreType.DMA((blocks, 2))

    def vmem(*arrays):
        return [(a, VMEM) for a in arrays]

    count = [(counts, SMEM)]
    kept, given, k, v, q = call(
        state_kernel, count + [(key_rows, HBM), (values, HBM), (queries, HBM)],
        [keep, give, half, half, half], unit, [pltpu.SemaphoreType.DMA((3,))])
    cover = call(
        score_kernel, count + [(cotangent, HBM)] + vmem(q, k, v),
        [plane, square, states, half], 7 * unit, [pltpu.SemaphoreType.DMA((1,))])
    near, far, _, (part, turned, run, cot) = outside_sum(kept, given, False, [], cover)
    grad, prefix, back, kept, given = call(
        norm_kernel, count + vmem(q, cot, out_gain.reshape(1, width), part, run, near, far),
        [half, prefixes, states, keep, give], 2 * unit)
    core_cover = call(value_kernel, vmem(grad, turned), [plane], 2 * unit)
    cover = call(
        pull_kernel, vmem(q, k, v, grad, prefix), [result, plane], 9 * unit,
        [staged, pltpu.SemaphoreType.DMA((1,))])
    near, far, (gv_part,), (gq, gk_part) = outside_sum(kept, given, True, core_cover, cover)
    gk, gv = call(
        final_kernel, count + vmem(k, v, gk_part, gv_part, back, near, far), [result, result], 2 * unit,
        [staged, staged, pair_sems])
    return gq, gk, gv


def solution(mesh):
    rows = P(("groups", "seq", "loader"), "head")
    return jax.shard_map(
        shards,
        mesh=mesh,
        in_specs=(rows, rows, rows, rows, P("head"), P(("groups", "seq", "loader"))),
        out_specs=(rows, rows, rows),
        check_vma=False,
    )
```

```python
import functools
import math

import jax
import jax.numpy as jnp
from jax import lax
from jax.experimental import pallas as pl
from jax.experimental.pallas import tpu as pltpu
from jax.sharding import PartitionSpec as P

DH = 128
SPAN = 256
LIVE = 6
EPSILON = 1e-06
F32 = jnp.float32
BF16 = jnp.bfloat16
VMEM = pl.BlockSpec(memory_space=pltpu.VMEM)
SMEM = pl.BlockSpec(memory_space=pltpu.SMEM)
HBM = pl.BlockSpec(memory_space=pltpu.HBM)
SWAP = [(0, 1), (1, 0)]


def nn(a, b):
    return lax.dot_general(a, b, (((1,), (0,)), ((), ())), preferred_element_type=F32)


def nt(a, b):
    return lax.dot_general(a, b, (((1,), (1,)), ((), ())), preferred_element_type=F32)


def tn(a, b):
    return lax.dot_general(a, b, (((0,), (0,)), ((), ())), preferred_element_type=F32)


def rows_of(block):
    if isinstance(block, int):
        return slice(block * SPAN, (block + 1) * SPAN)
    return pl.ds(pl.multiple_of(block * SPAN, SPAN), SPAN)


def columns_of(core):
    return pl.ds(pl.multiple_of(core * DH, DH), DH)


def fetch(pairs, sems):
    copies = [pltpu.make_async_copy(source, target, sems.at[at]) for at, (source, target) in enumerate(pairs)]
    for copy in copies:
        copy.start()
    return copies


def wait(copies):
    for copy in copies:
        copy.wait()


def core_and_counts(count_ref):
    core, own = lax.axis_index("loader"), count_ref[0]
    return core, jnp.where(core == 0, own, LIVE - own), own


def live_block(own_ref, other_ref, at, core, count):
    late = (at >= count).astype(jnp.int32)
    r = rows_of(at - late * count)
    c = columns_of(core) if other_ref.shape[1] > DH else slice(None)
    return jnp.where(late == core, own_ref[r, :], other_ref[r, c])


def load_kernel(k_hbm, v_hbm, q_hbm, cot_hbm, gain_hbm,
                k_ref, v_ref, q_ref, cot_ref, give_ref, gain_ref, sems):
    core = lax.axis_index("loader")
    own, other = columns_of(core), columns_of(1 - core)
    wait(fetch(((k_hbm.at[:, own], k_ref), (v_hbm.at[:, own], v_ref), (q_hbm.at[:, own], q_ref),
                (cot_hbm.at[:, own], cot_ref), (q_hbm.at[:, other], give_ref.at[0]),
                (cot_hbm.at[:, other], give_ref.at[1]), (gain_hbm, gain_ref)), sems))


def state_kernel(count_ref, k_own_ref, v_own_ref, k_other_ref, v_other_ref, total_ref, k_ref, v_ref, run_ref):
    core, count, _ = core_and_counts(count_ref)
    running = jnp.zeros((DH, DH), F32)
    for at in range(LIVE):
        r = rows_of(at)
        k = live_block(k_own_ref, k_other_ref, at, core, count)
        v = live_block(v_own_ref, v_other_ref, at, core, count)
        k_ref[r, :], v_ref[r, :] = k, v
        run_ref[at] = running
        running = running + tn(k, v)
    total_ref[...] = running.astype(total_ref.dtype)


def score_kernel(count_ref, q_own_ref, cot_own_ref, other_ref, k_ref, v_ref,
                 q_ref, cot_ref, part_ref, turned_ref):
    core, count, _ = core_and_counts(count_ref)
    t = lax.broadcasted_iota(jnp.int32, (SPAN, SPAN), 0)
    s = lax.broadcasted_iota(jnp.int32, (SPAN, SPAN), 1)
    for at in range(LIVE):
        r = rows_of(at)
        q = live_block(q_own_ref, other_ref.at[0], at, core, count)
        q_ref[r, :] = q
        cot_ref[r, :] = live_block(cot_own_ref, other_ref.at[1], at, core, count)
        k = k_ref[r, :]
        scored = jnp.where(t >= s, nt(q, k), 0.0).astype(BF16)
        part_ref[r, :] = nn(scored, v_ref[r, :])
        turned_ref[at] = jnp.where(t <= s, nt(k, q), 0.0).astype(BF16)


def norm_kernel(q_ref, cot_ref, gain_ref, part_ref, run_ref, outside_ref,
                grad_ref, prefix_ref, back_ref, total_ref):
    outside = outside_ref[...]
    gain = gain_ref[:, columns_of(lax.axis_index("loader"))]
    running = jnp.zeros((DH, DH), F32)
    for at in reversed(range(LIVE)):
        r = rows_of(at)
        prefix = (run_ref[at] + outside).astype(BF16)
        prefix_ref[at] = prefix
        q = q_ref[r, :]
        raw = part_ref[r, :] + nn(q, prefix)
        inverse = lax.rsqrt(jnp.mean(raw * raw, axis=-1, keepdims=True) + EPSILON)
        weighted = gain * cot_ref[r, :].astype(F32)
        pulled = jnp.mean(weighted * raw, axis=-1, keepdims=True)
        grad = (inverse * weighted - raw * (inverse * inverse * inverse * pulled)).astype(BF16)
        grad_ref[r, :] = grad
        back_ref[at] = running
        running = running + tn(q, grad)
    total_ref[...] = running.astype(total_ref.dtype)


def spread(live_ref, own_ref, other_ref, core, count, own):
    for b in range(own_ref.shape[0] // SPAN):
        for target, shift, limit in (
                (own_ref, jnp.where(core == 0, 0, count), own),
                (other_ref, jnp.where(core == 0, count, 0), LIVE - own)):
            block = live_ref[rows_of(jnp.minimum(b + shift, LIVE - 1)), :]
            target[rows_of(b), :] = jnp.where(b < limit, block, jnp.zeros_like(block))


def pull_kernel(count_ref, q_ref, k_ref, v_ref, grad_ref, turned_ref, prefix_ref,
                gq_own_ref, other_ref, gk_ref, gv_ref, gq_ref):
    t = lax.broadcasted_iota(jnp.int32, (SPAN, SPAN), 0)
    s = lax.broadcasted_iota(jnp.int32, (SPAN, SPAN), 1)
    for at in range(LIVE):
        r = rows_of(at)
        v, grad = v_ref[r, :], grad_ref[r, :]
        pull = jnp.where(t >= s, nt(grad, v), 0.0).astype(BF16)
        gq_ref[r, :] = (nn(pull, k_ref[r, :]) + nt(grad, prefix_ref[at])).astype(BF16)
        turned = jnp.where(t <= s, nt(v, grad), 0.0).astype(BF16)
        gk_ref[r, :] = nn(turned, q_ref[r, :])
        gv_ref[r, :] = nn(turned_ref[at], grad)
    spread(gq_ref, gq_own_ref, other_ref.at[0], *core_and_counts(count_ref))


def suffix_kernel(count_ref, k_ref, v_ref, gk_part_ref, gv_part_ref, back_ref, outside_ref, begun_ref,
                  gk_own_ref, gv_own_ref, other_ref, gk_ref, gv_ref):
    del begun_ref
    outside = outside_ref[...]
    for at in range(LIVE):
        r = rows_of(at)
        suffix = (back_ref[at] + outside).astype(BF16)
        gk_ref[r, :] = (gk_part_ref[r, :] + nt(v_ref[r, :], suffix)).astype(BF16)
        gv_ref[r, :] = (gv_part_ref[r, :] + nn(k_ref[r, :], suffix)).astype(BF16)
    where = core_and_counts(count_ref)
    spread(gk_ref, gk_own_ref, other_ref.at[1], *where)
    spread(gv_ref, gv_own_ref, other_ref.at[2], *where)


def own_kernel(gq_own_ref, gk_own_ref, gv_own_ref, gq_hbm, gk_hbm, gv_hbm, sems):
    c = columns_of(lax.axis_index("loader"))
    wait(fetch(((gq_own_ref, gq_hbm.at[:, c]), (gk_own_ref, gk_hbm.at[:, c]), (gv_own_ref, gv_hbm.at[:, c])), sems))


def came_kernel(came_ref, gq_in_hbm, gk_in_hbm, gv_in_hbm, gq_hbm, gk_hbm, gv_hbm, sems):
    del gq_in_hbm, gk_in_hbm, gv_in_hbm
    c = columns_of(1 - lax.axis_index("loader"))
    wait(fetch([(came_ref.at[at], target.at[:, c]) for at, target in enumerate((gq_hbm, gk_hbm, gv_hbm))], sems))


def call(kernel, ins, outs, flops, scratch=(), aliases={}):
    size = sum(a.size * a.dtype.itemsize for a, _ in ins)
    size += sum(math.prod(shape) * jnp.dtype(kind).itemsize for (shape, kind), _ in outs)
    return pl.pallas_call(
        kernel,
        out_shape=[pltpu.VMEM(*a) if space is VMEM else pltpu.HBM(*a) for a, space in outs],
        in_specs=[space for _, space in ins],
        out_specs=[space for _, space in outs],
        scratch_shapes=scratch,
        input_output_aliases=aliases,
        cost_estimate=pl.CostEstimate(flops=flops, bytes_accessed=size, transcendentals=0),
        compiler_params=pltpu.CompilerParams(vmem_limit_bytes=16 * 2**20),
    )(*[a if space is SMEM else pltpu.with_memory_space_constraint(a, space.memory_space) for a, space in ins])


def radices(count):
    found = []
    for radix in (4, 2):
        while count % radix == 0:
            found.append(radix)
            count //= radix
    return found + [count] if count > 1 else found


def partner(digit, step, radix):
    return digit ^ step if radix in (2, 4) else (digit + step) % radix


def combine_kernel(steps, radix, stride, reverse, first, last, *refs):
    group_ref, came, outs = refs[0], refs[1:1 + len(steps)], refs[1 + len(steps) + (not first):]
    digit = lax.rem(lax.div(lax.axis_index("seq"), stride), radix)
    outside = jnp.zeros(outs[0].shape, F32) if first else refs[1 + len(steps)][...]
    whole = group_ref[...].astype(F32)
    for step, piece_ref in zip(steps, came):
        source = partner(digit, step if radix in (2, 4) else radix - step, radix)
        use = source > digit if reverse else source < digit
        piece = piece_ref[...].astype(F32)
        outside = outside + jnp.where(use, piece, 0.0)
        whole = whole + piece
    outs[0][...] = outside
    if not last:
        outs[1][...] = whole.astype(outs[1].dtype)


def order(radix, reverse):
    return [3, 2, 1] if radix == 4 else list(range(radix - 1, 0, -1))


def outside_sum(total, reverse, cover):
    count, stride, group, outside = lax.axis_size("seq"), 1, total, []
    chain = radices(count)
    for at, radix in enumerate(chain):
        steps = order(radix, reverse)
        came = []
        for step in steps:
            pairs = [(s, s + (partner(s // stride % radix, step, radix) - s // stride % radix) * stride)
                     for s in range(count)]
            came.append(lax.ppermute(group, "seq", pairs))
        if at == 0:
            came, cover = lax.optimization_barrier((came, cover))
        last = at + 1 == len(chain)
        kernel = functools.partial(combine_kernel, steps, radix, stride, reverse, at == 0, last)
        sums = [((total.shape, F32), VMEM)] + ([] if last else [((total.shape, total.dtype), VMEM)])
        out = call(kernel, [(a, VMEM) for a in (group, *came, *outside)], sums, total.size)
        outside, group = out[:1], out[-1]
        stride *= radix
    return outside[0], cover


def shards(queries, key_rows, values, cotangent, out_gain, counts):
    rows, width = queries.shape
    unit = 2 * LIVE * SPAN * DH * DH
    buffer = ((rows, DH), BF16), VMEM
    half = ((LIVE * SPAN, DH), BF16), VMEM
    plane = ((LIVE * SPAN, DH), F32), VMEM
    states = ((LIVE, DH, DH), F32), VMEM
    prefixes = ((LIVE, DH, DH), BF16), VMEM
    total = ((DH, DH), BF16), VMEM
    square = ((LIVE, SPAN, SPAN), BF16), VMEM
    result = ((rows, width), BF16), HBM
    staged = pltpu.VMEM((LIVE * SPAN, DH), BF16)
    count = [(counts, SMEM)]

    def vmem(*arrays):
        return [(a, VMEM) for a in arrays]

    def sems(n):
        return pltpu.SemaphoreType.DMA((n,))

    def swap(array):
        return lax.ppermute(array, "loader", SWAP)

    k_other, v_other = swap(key_rows), swap(values)
    pair = ((2, rows, DH), BF16), VMEM
    loaded = call(
        load_kernel, [(a, HBM) for a in (key_rows, values, queries, cotangent, out_gain.reshape(1, width))],
        [buffer] * 4 + [pair, (((1, width), F32), VMEM)], 0, [sems(7)])
    k_other, v_other, loaded = lax.optimization_barrier((k_other, v_other, loaded))
    k_own, v_own, q_own, cot_own, give, gain = loaded
    own, k, v, run = call(
        state_kernel, count + vmem(k_own, v_own, k_other, v_other), [total, half, half, states], unit)
    cover = call(
        score_kernel, count + vmem(q_own, cot_own, swap(give), k, v), [half, half, plane, square], 6 * unit)
    outside, (q, cot, part, turned) = outside_sum(own, False, cover)
    grad, prefix, back, own_back = call(
        norm_kernel, vmem(q, cot, gain, part, run, outside),
        [half, prefixes, states, total], 2 * unit)
    three = ((3, rows, DH), BF16), VMEM
    cover = call(
        pull_kernel, count + vmem(q, k, v, grad, turned, prefix), [buffer, three, plane, plane], 11 * unit, [staged])
    outside, (gq_own, other, gk_part, gv_part) = outside_sum(own_back, True, cover)
    gk_own, gv_own, other = call(
        suffix_kernel, count + vmem(k, v, gk_part, gv_part, back, outside, other),
        [buffer, buffer, three], 2 * unit, [staged, staged], {7: 2})
    came = swap(other)
    grads = call(own_kernel, vmem(gq_own, gk_own, gv_own), [result] * 3, 0, [sems(3)])
    came, grads = lax.optimization_barrier((came, grads))
    return tuple(call(
        came_kernel, vmem(came) + [(grad, HBM) for grad in grads], [result] * 3, 0, [sems(3)], {1: 0, 2: 1, 3: 2}))


def solution(mesh):
    rows = P(("groups", "seq", "loader"), "head")
    return jax.shard_map(
        shards,
        mesh=mesh,
        in_specs=(rows, rows, rows, rows, P("head"), P(("groups", "seq", "loader"))),
        out_specs=(rows, rows, rows),
        check_vma=False,
    )
```

```python
import functools
import math

import jax
import jax.numpy as jnp
from jax import lax
from jax.experimental import pallas as pl
from jax.experimental.pallas import tpu as pltpu
from jax.sharding import PartitionSpec as P

DH = 128
SPAN = 256
LIVE = 6
EPSILON = 1e-06
F32 = jnp.float32
BF16 = jnp.bfloat16
VMEM = pl.BlockSpec(memory_space=pltpu.VMEM)
SMEM = pl.BlockSpec(memory_space=pltpu.SMEM)
HBM = pl.BlockSpec(memory_space=pltpu.HBM)
SWAP = [(0, 1), (1, 0)]


def nn(a, b):
    return lax.dot_general(a, b, (((1,), (0,)), ((), ())), preferred_element_type=F32)


def nt(a, b):
    return lax.dot_general(a, b, (((1,), (1,)), ((), ())), preferred_element_type=F32)


def tn(a, b):
    return lax.dot_general(a, b, (((0,), (0,)), ((), ())), preferred_element_type=F32)


def rows_of(block):
    if isinstance(block, int):
        return slice(block * SPAN, (block + 1) * SPAN)
    return pl.ds(pl.multiple_of(block * SPAN, SPAN), SPAN)


def columns_of(core):
    return pl.ds(pl.multiple_of(core * DH, DH), DH)


def fetch(pairs, sems):
    copies = [pltpu.make_async_copy(source, target, sems.at[at]) for at, (source, target) in enumerate(pairs)]
    for copy in copies:
        copy.start()
    return copies


def wait(copies):
    for copy in copies:
        copy.wait()


def core_and_counts(count_ref):
    core, own = lax.axis_index("loader"), count_ref[0]
    return core, jnp.where(core == 0, own, LIVE - own), own


def live_block(own_ref, other_ref, at, core, count):
    late = (at >= count).astype(jnp.int32)
    r = rows_of(at - late * count)
    return jnp.where(late == core, own_ref[r, :], other_ref[r, :])


def give_kernel(k_hbm, v_hbm, give_ref, sems):
    other = columns_of(1 - lax.axis_index("loader"))
    wait(fetch([(source.at[:, other], give_ref.at[at]) for at, source in enumerate((k_hbm, v_hbm))], sems))


def load_kernel(count_ref, k_hbm, v_hbm, q_hbm, cot_hbm, gain_hbm,
                k_ref, v_ref, q_ref, cot_ref, give_ref, gain_ref, sems):
    del count_ref
    core = lax.axis_index("loader")
    own, other = columns_of(core), columns_of(1 - core)
    wait(fetch(((k_hbm.at[:, own], k_ref), (v_hbm.at[:, own], v_ref), (q_hbm.at[:, own], q_ref),
                (cot_hbm.at[:, own], cot_ref), (q_hbm.at[:, other], give_ref.at[0]),
                (cot_hbm.at[:, other], give_ref.at[1]), (gain_hbm, gain_ref)), sems))


def state_kernel(count_ref, k_own_ref, v_own_ref, other_ref, total_ref, k_ref, v_ref, run_ref):
    core, count, _ = core_and_counts(count_ref)
    running = jnp.zeros((DH, DH), F32)
    for at in range(LIVE):
        r = rows_of(at)
        k = live_block(k_own_ref, other_ref.at[0], at, core, count)
        v = live_block(v_own_ref, other_ref.at[1], at, core, count)
        k_ref[r, :], v_ref[r, :] = k, v
        run_ref[at] = running
        running = running + tn(k, v)
    total_ref[...] = running.astype(total_ref.dtype)


def score_kernel(count_ref, q_own_ref, cot_own_ref, other_ref, k_ref, v_ref,
                 q_ref, cot_ref, part_ref, turned_ref):
    core, count, _ = core_and_counts(count_ref)
    t = lax.broadcasted_iota(jnp.int32, (SPAN, SPAN), 0)
    s = lax.broadcasted_iota(jnp.int32, (SPAN, SPAN), 1)
    for at in range(LIVE):
        r = rows_of(at)
        q = live_block(q_own_ref, other_ref.at[0], at, core, count)
        q_ref[r, :] = q
        cot_ref[r, :] = live_block(cot_own_ref, other_ref.at[1], at, core, count)
        k = k_ref[r, :]
        scored = jnp.where(t >= s, nt(q, k), 0.0).astype(BF16)
        part_ref[r, :] = nn(scored, v_ref[r, :])
        turned_ref[at] = jnp.where(t <= s, nt(k, q), 0.0).astype(BF16)


def norm_kernel(q_ref, cot_ref, gain_ref, part_ref, run_ref, outside_ref,
                grad_ref, prefix_ref, back_ref, total_ref):
    outside = outside_ref[...]
    gain = gain_ref[:, columns_of(lax.axis_index("loader"))]
    running = jnp.zeros((DH, DH), F32)
    for at in reversed(range(LIVE)):
        r = rows_of(at)
        prefix = (run_ref[at] + outside).astype(BF16)
        prefix_ref[at] = prefix
        q = q_ref[r, :]
        raw = part_ref[r, :] + nn(q, prefix)
        inverse = lax.rsqrt(jnp.mean(raw * raw, axis=-1, keepdims=True) + EPSILON)
        weighted = gain * cot_ref[r, :].astype(F32)
        pulled = jnp.mean(weighted * raw, axis=-1, keepdims=True)
        grad = (inverse * weighted - raw * (inverse * inverse * inverse * pulled)).astype(BF16)
        grad_ref[r, :] = grad
        back_ref[at] = running
        running = running + tn(q, grad)
    total_ref[...] = running.astype(total_ref.dtype)


def spread(live_ref, own_ref, other_ref, core, count, own):
    for b in range(own_ref.shape[0] // SPAN):
        for target, shift, limit in (
                (own_ref, jnp.where(core == 0, 0, count), own),
                (other_ref, jnp.where(core == 0, count, 0), LIVE - own)):
            block = live_ref[rows_of(jnp.minimum(b + shift, LIVE - 1)), :]
            target[rows_of(b), :] = jnp.where(b < limit, block, jnp.zeros_like(block))


def pull_kernel(count_ref, q_ref, k_ref, v_ref, grad_ref, turned_ref, prefix_ref,
                gq_own_ref, other_ref, gk_ref, gv_ref, gq_ref):
    t = lax.broadcasted_iota(jnp.int32, (SPAN, SPAN), 0)
    s = lax.broadcasted_iota(jnp.int32, (SPAN, SPAN), 1)
    for at in range(LIVE):
        r = rows_of(at)
        v, grad = v_ref[r, :], grad_ref[r, :]
        pull = jnp.where(t >= s, nt(grad, v), 0.0).astype(BF16)
        gq_ref[r, :] = (nn(pull, k_ref[r, :]) + nt(grad, prefix_ref[at])).astype(BF16)
        turned = jnp.where(t <= s, nt(v, grad), 0.0).astype(BF16)
        gk_ref[r, :] = nn(turned, q_ref[r, :])
        gv_ref[r, :] = nn(turned_ref[at], grad)
    spread(gq_ref, gq_own_ref, other_ref.at[0], *core_and_counts(count_ref))


def suffix_kernel(count_ref, k_ref, v_ref, gk_part_ref, gv_part_ref, back_ref, outside_ref, begun_ref,
                  gk_own_ref, gv_own_ref, other_ref, gk_ref, gv_ref):
    del begun_ref
    outside = outside_ref[...]
    for at in range(LIVE):
        r = rows_of(at)
        suffix = (back_ref[at] + outside).astype(BF16)
        gk_ref[r, :] = (gk_part_ref[r, :] + nt(v_ref[r, :], suffix)).astype(BF16)
        gv_ref[r, :] = (gv_part_ref[r, :] + nn(k_ref[r, :], suffix)).astype(BF16)
    where = core_and_counts(count_ref)
    spread(gk_ref, gk_own_ref, other_ref.at[1], *where)
    spread(gv_ref, gv_own_ref, other_ref.at[2], *where)


def own_kernel(gq_own_ref, gk_own_ref, gv_own_ref, gq_hbm, gk_hbm, gv_hbm, sems):
    c = columns_of(lax.axis_index("loader"))
    wait(fetch(((gq_own_ref, gq_hbm.at[:, c]), (gk_own_ref, gk_hbm.at[:, c]), (gv_own_ref, gv_hbm.at[:, c])), sems))


def came_kernel(came_ref, gq_in_hbm, gk_in_hbm, gv_in_hbm, gq_hbm, gk_hbm, gv_hbm, sems):
    del gq_in_hbm, gk_in_hbm, gv_in_hbm
    c = columns_of(1 - lax.axis_index("loader"))
    wait(fetch([(came_ref.at[at], target.at[:, c]) for at, target in enumerate((gq_hbm, gk_hbm, gv_hbm))], sems))


def call(kernel, ins, outs, flops, scratch=(), aliases={}):
    size = sum(a.size * a.dtype.itemsize for a, _ in ins)
    size += sum(math.prod(shape) * jnp.dtype(kind).itemsize for (shape, kind), _ in outs)
    return pl.pallas_call(
        kernel,
        out_shape=[pltpu.VMEM(*a) if space is VMEM else pltpu.HBM(*a) for a, space in outs],
        in_specs=[space for _, space in ins],
        out_specs=[space for _, space in outs],
        scratch_shapes=scratch,
        input_output_aliases=aliases,
        cost_estimate=pl.CostEstimate(flops=flops, bytes_accessed=size, transcendentals=0),
        compiler_params=pltpu.CompilerParams(vmem_limit_bytes=16 * 2**20),
    )(*[a if space is SMEM else pltpu.with_memory_space_constraint(a, space.memory_space) for a, space in ins])


def radices(count):
    found = []
    for radix in (4, 2):
        while count % radix == 0:
            found.append(radix)
            count //= radix
    return found + [count] if count > 1 else found


def partner(digit, step, radix):
    return digit ^ step if radix in (2, 4) else (digit + step) % radix


def combine_kernel(steps, radix, stride, reverse, first, last, *refs):
    group_ref, came, outs = refs[0], refs[1:1 + len(steps)], refs[1 + len(steps) + (not first):]
    digit = lax.rem(lax.div(lax.axis_index("seq"), stride), radix)
    outside = jnp.zeros(outs[0].shape, F32) if first else refs[1 + len(steps)][...]
    whole = group_ref[...].astype(F32)
    for step, piece_ref in zip(steps, came):
        source = partner(digit, step if radix in (2, 4) else radix - step, radix)
        use = source > digit if reverse else source < digit
        piece = piece_ref[...].astype(F32)
        outside = outside + jnp.where(use, piece, 0.0)
        whole = whole + piece
    outs[0][...] = outside
    if not last:
        outs[1][...] = whole.astype(outs[1].dtype)


def order(radix, reverse):
    return [3, 2, 1] if radix == 4 else list(range(radix - 1, 0, -1))


def outside_sum(total, reverse, cover):
    count, stride, group, outside = lax.axis_size("seq"), 1, total, []
    chain = radices(count)
    for at, radix in enumerate(chain):
        steps = order(radix, reverse)
        came = []
        for step in steps:
            pairs = [(s, s + (partner(s // stride % radix, step, radix) - s // stride % radix) * stride)
                     for s in range(count)]
            came.append(lax.ppermute(group, "seq", pairs))
        if at == 0:
            came, cover = lax.optimization_barrier((came, cover))
        last = at + 1 == len(chain)
        kernel = functools.partial(combine_kernel, steps, radix, stride, reverse, at == 0, last)
        sums = [((total.shape, F32), VMEM)] + ([] if last else [((total.shape, total.dtype), VMEM)])
        out = call(kernel, [(a, VMEM) for a in (group, *came, *outside)], sums, total.size)
        outside, group = out[:1], out[-1]
        stride *= radix
    return outside[0], cover


def shards(queries, key_rows, values, cotangent, out_gain, counts):
    rows, width = queries.shape
    unit = 2 * LIVE * SPAN * DH * DH
    buffer = ((rows, DH), BF16), VMEM
    half = ((LIVE * SPAN, DH), BF16), VMEM
    plane = ((LIVE * SPAN, DH), F32), VMEM
    states = ((LIVE, DH, DH), F32), VMEM
    prefixes = ((LIVE, DH, DH), BF16), VMEM
    total = ((DH, DH), BF16), VMEM
    square = ((LIVE, SPAN, SPAN), BF16), VMEM
    result = ((rows, width), BF16), HBM
    staged = pltpu.VMEM((LIVE * SPAN, DH), BF16)
    count = [(counts, SMEM)]

    def vmem(*arrays):
        return [(a, VMEM) for a in arrays]

    def sems(n):
        return pltpu.SemaphoreType.DMA((n,))

    def swap(array):
        return lax.ppermute(array, "loader", SWAP)

    pair = ((2, rows, DH), BF16), VMEM
    give, = call(give_kernel, [(key_rows, HBM), (values, HBM)], [pair], 0, [sems(2)])
    other = swap(give)
    loaded = call(
        load_kernel, count + [(a, HBM) for a in (key_rows, values, queries, cotangent, out_gain.reshape(1, width))],
        [buffer] * 4 + [pair, (((1, width), F32), VMEM)], 0, [sems(7)])
    other, (k_own, v_own, q_own, cot_own, give, gain) = lax.optimization_barrier((other, loaded))
    own, k, v, run = call(
        state_kernel, count + vmem(k_own, v_own, other), [total, half, half, states], unit)
    cover = call(
        score_kernel, count + vmem(q_own, cot_own, swap(give), k, v), [half, half, plane, square], 6 * unit)
    outside, (q, cot, part, turned) = outside_sum(own, False, cover)
    grad, prefix, back, own_back = call(
        norm_kernel, vmem(q, cot, gain, part, run, outside),
        [half, prefixes, states, total], 2 * unit)
    three = ((3, rows, DH), BF16), VMEM
    cover = call(
        pull_kernel, count + vmem(q, k, v, grad, turned, prefix), [buffer, three, plane, plane], 11 * unit, [staged])
    outside, (gq_own, other, gk_part, gv_part) = outside_sum(own_back, True, cover)
    gk_own, gv_own, other = call(
        suffix_kernel, count + vmem(k, v, gk_part, gv_part, back, outside, other),
        [buffer, buffer, three], 2 * unit, [staged, staged], {7: 2})
    came = swap(other)
    grads = call(own_kernel, vmem(gq_own, gk_own, gv_own), [result] * 3, 0, [sems(3)])
    came, grads = lax.optimization_barrier((came, grads))
    return tuple(call(
        came_kernel, vmem(came) + [(grad, HBM) for grad in grads], [result] * 3, 0, [sems(3)], {1: 0, 2: 1, 3: 2}))


def solution(mesh):
    rows = P(("groups", "seq", "loader"), "head")
    return jax.shard_map(
        shards,
        mesh=mesh,
        in_specs=(rows, rows, rows, rows, P("head"), P(("groups", "seq", "loader"))),
        out_specs=(rows, rows, rows),
        check_vma=False,
    )
```

```python
import functools
import math

import jax
import jax.numpy as jnp
from jax import lax
from jax.experimental import pallas as pl
from jax.experimental.pallas import tpu as pltpu
from jax.sharding import PartitionSpec as P

DH = 128
SPAN = 256
LIVE = 6
EPSILON = 1e-06
COVER = 10**10
F32 = jnp.float32
BF16 = jnp.bfloat16
VMEM = pl.BlockSpec(memory_space=pltpu.VMEM)
SMEM = pl.BlockSpec(memory_space=pltpu.SMEM)
HBM = pl.BlockSpec(memory_space=pltpu.HBM)
SWAP = [(0, 1), (1, 0)]


def nn(a, b):
    return lax.dot_general(a, b, (((1,), (0,)), ((), ())), preferred_element_type=F32)


def nt(a, b):
    return lax.dot_general(a, b, (((1,), (1,)), ((), ())), preferred_element_type=F32)


def tn(a, b):
    return lax.dot_general(a, b, (((0,), (0,)), ((), ())), preferred_element_type=F32)


def rows_of(block):
    if isinstance(block, int):
        return slice(block * SPAN, (block + 1) * SPAN)
    return pl.ds(pl.multiple_of(block * SPAN, SPAN), SPAN)


def columns_of(core):
    return pl.ds(pl.multiple_of(core * DH, DH), DH)


def fetch(pairs, sems):
    copies = [pltpu.make_async_copy(source, target, sems.at[at]) for at, (source, target) in enumerate(pairs)]
    for copy in copies:
        copy.start()
    return copies


def wait(copies):
    for copy in copies:
        copy.wait()


def core_and_counts(count_ref):
    core, own = lax.axis_index("loader"), count_ref[0]
    return core, jnp.where(core == 0, own, LIVE - own), own


def live_block(own_ref, other_ref, at, core, count):
    late = (at >= count).astype(jnp.int32)
    r = rows_of(at - late * count)
    return jnp.where(late == core, own_ref[r, :], other_ref[r, :])


def give_kernel(k_hbm, v_hbm, give_ref, sems):
    other = columns_of(1 - lax.axis_index("loader"))
    wait(fetch([(source.at[:, other], give_ref.at[at]) for at, source in enumerate((k_hbm, v_hbm))], sems))


def load_kernel(count_ref, k_hbm, v_hbm, q_hbm, cot_hbm, gain_hbm,
                k_ref, v_ref, q_ref, cot_ref, give_ref, gain_ref, sems):
    del count_ref
    core = lax.axis_index("loader")
    own, other = columns_of(core), columns_of(1 - core)
    wait(fetch(((k_hbm.at[:, own], k_ref), (v_hbm.at[:, own], v_ref), (q_hbm.at[:, own], q_ref),
                (cot_hbm.at[:, own], cot_ref), (q_hbm.at[:, other], give_ref.at[0]),
                (cot_hbm.at[:, other], give_ref.at[1]), (gain_hbm, gain_ref)), sems))


def state_kernel(count_ref, k_own_ref, v_own_ref, other_ref, total_ref, k_ref, v_ref, run_ref):
    core, count, _ = core_and_counts(count_ref)
    running = jnp.zeros((DH, DH), F32)
    for at in range(LIVE):
        r = rows_of(at)
        k = live_block(k_own_ref, other_ref.at[0], at, core, count)
        v = live_block(v_own_ref, other_ref.at[1], at, core, count)
        k_ref[r, :], v_ref[r, :] = k, v
        run_ref[at] = running
        running = running + tn(k, v)
    total_ref[...] = running.astype(total_ref.dtype)


def score_kernel(count_ref, q_own_ref, cot_own_ref, other_ref, k_ref, v_ref,
                 q_ref, cot_ref, part_ref, turned_ref):
    core, count, _ = core_and_counts(count_ref)
    t = lax.broadcasted_iota(jnp.int32, (SPAN, SPAN), 0)
    s = lax.broadcasted_iota(jnp.int32, (SPAN, SPAN), 1)
    for at in range(LIVE):
        r = rows_of(at)
        q = live_block(q_own_ref, other_ref.at[0], at, core, count)
        q_ref[r, :] = q
        cot_ref[r, :] = live_block(cot_own_ref, other_ref.at[1], at, core, count)
        k = k_ref[r, :]
        scored = jnp.where(t >= s, nt(q, k), 0.0).astype(BF16)
        part_ref[r, :] = nn(scored, v_ref[r, :])
        turned_ref[at] = jnp.where(t <= s, nt(k, q), 0.0).astype(BF16)


def norm_kernel(q_ref, cot_ref, gain_ref, part_ref, run_ref, outside_ref,
                grad_ref, prefix_ref, back_ref, total_ref):
    outside = outside_ref[...]
    gain = gain_ref[:, columns_of(lax.axis_index("loader"))]
    running = jnp.zeros((DH, DH), F32)
    for at in reversed(range(LIVE)):
        r = rows_of(at)
        prefix = (run_ref[at] + outside).astype(BF16)
        prefix_ref[at] = prefix
        q = q_ref[r, :]
        raw = part_ref[r, :] + nn(q, prefix)
        inverse = lax.rsqrt(jnp.mean(raw * raw, axis=-1, keepdims=True) + EPSILON)
        weighted = gain * cot_ref[r, :].astype(F32)
        pulled = jnp.mean(weighted * raw, axis=-1, keepdims=True)
        grad = (inverse * weighted - raw * (inverse * inverse * inverse * pulled)).astype(BF16)
        grad_ref[r, :] = grad
        back_ref[at] = running
        running = running + tn(q, grad)
    total_ref[...] = running.astype(total_ref.dtype)


def spread(live_ref, own_ref, other_ref, core, count, own):
    for b in range(own_ref.shape[0] // SPAN):
        for target, shift, limit in (
                (own_ref, jnp.where(core == 0, 0, count), own),
                (other_ref, jnp.where(core == 0, count, 0), LIVE - own)):
            block = live_ref[rows_of(jnp.minimum(b + shift, LIVE - 1)), :]
            target[rows_of(b), :] = jnp.where(b < limit, block, jnp.zeros_like(block)).astype(target.dtype)


def pull_kernel(count_ref, q_ref, k_ref, v_ref, grad_ref, turned_ref, prefix_ref, back_ref,
                gq_own_ref, own_ref, other_ref, gq_ref, gk_ref, gv_ref):
    t = lax.broadcasted_iota(jnp.int32, (SPAN, SPAN), 0)
    s = lax.broadcasted_iota(jnp.int32, (SPAN, SPAN), 1)
    for at in range(LIVE):
        r = rows_of(at)
        k, v, grad, back = k_ref[r, :], v_ref[r, :], grad_ref[r, :], back_ref[at].astype(BF16)
        pull = jnp.where(t >= s, nt(grad, v), 0.0).astype(BF16)
        gq_ref[r, :] = (nn(pull, k) + nt(grad, prefix_ref[at])).astype(BF16)
        turned = jnp.where(t <= s, nt(v, grad), 0.0).astype(BF16)
        gk_ref[r, :] = nn(turned, q_ref[r, :]) + nt(v, back)
        gv_ref[r, :] = nn(turned_ref[at], grad) + nn(k, back)
    where = core_and_counts(count_ref)
    spread(gq_ref, gq_own_ref, other_ref.at[0], *where)
    spread(gk_ref, own_ref.at[0], other_ref.at[1], *where)
    spread(gv_ref, own_ref.at[1], other_ref.at[2], *where)


def final_kernel(count_ref, gq_own_ref, own_ref, k_own_ref, v_own_ref, outside_ref,
                 came_ref, give_ref, outside_came_ref, gq_hbm, gk_hbm, gv_hbm, gk_ref, gv_ref, sems):
    core, _, own = core_and_counts(count_ref)
    columns = columns_of(core), columns_of(1 - core)
    copies = fetch(((gq_own_ref, gq_hbm.at[:, columns[0]]), (came_ref.at[0], gq_hbm.at[:, columns[1]])), sems.at[0])
    heads = ((k_own_ref, v_own_ref, own_ref.at[0], own_ref.at[1], outside_ref),
             (give_ref.at[0], give_ref.at[1], came_ref.at[1], came_ref.at[2], outside_came_ref))
    for h, (k_ref, v_ref, gk_part_ref, gv_part_ref, sum_ref) in enumerate(heads):
        outside = sum_ref[...].astype(BF16)
        for b in range(k_ref.shape[0] // SPAN):
            r = rows_of(b)
            suffix = jnp.where(b < own, outside, jnp.zeros_like(outside))
            gk_ref[h, r, :] = (gk_part_ref[r, :].astype(F32) + nt(v_ref[r, :], suffix)).astype(BF16)
            gv_ref[h, r, :] = (gv_part_ref[r, :].astype(F32) + nn(k_ref[r, :], suffix)).astype(BF16)
        copies += fetch(((gk_ref.at[h], gk_hbm.at[:, columns[h]]), (gv_ref.at[h], gv_hbm.at[:, columns[h]])),
                        sems.at[1 + h])
    wait(copies)


def call(kernel, ins, outs, flops, scratch=(), aliases={}):
    size = sum(a.size * a.dtype.itemsize for a, _ in ins)
    size += sum(math.prod(shape) * jnp.dtype(kind).itemsize for (shape, kind), _ in outs)
    return pl.pallas_call(
        kernel,
        out_shape=[pltpu.VMEM(*a) if space is VMEM else pltpu.HBM(*a) for a, space in outs],
        in_specs=[space for _, space in ins],
        out_specs=[space for _, space in outs],
        scratch_shapes=scratch,
        input_output_aliases=aliases,
        cost_estimate=pl.CostEstimate(flops=flops, bytes_accessed=size, transcendentals=0),
        compiler_params=pltpu.CompilerParams(vmem_limit_bytes=16 * 2**20),
    )(*[a if space is SMEM else pltpu.with_memory_space_constraint(a, space.memory_space) for a, space in ins])


def radices(count):
    found = []
    for radix in (4, 2):
        while count % radix == 0:
            found.append(radix)
            count //= radix
    return found + [count] if count > 1 else found


def partner(digit, step, radix):
    return digit ^ step if radix in (2, 4) else (digit + step) % radix


def combine_kernel(steps, radix, stride, reverse, first, last, *refs):
    group_ref, came, outs = refs[0], refs[1:1 + len(steps)], refs[1 + len(steps) + (not first):]
    digit = lax.rem(lax.div(lax.axis_index("seq"), stride), radix)
    outside = jnp.zeros(outs[0].shape, F32) if first else refs[1 + len(steps)][...]
    whole = group_ref[...].astype(F32)
    for step, piece_ref in zip(steps, came):
        source = partner(digit, step if radix in (2, 4) else radix - step, radix)
        use = source > digit if reverse else source < digit
        piece = piece_ref[...].astype(F32)
        outside = outside + jnp.where(use, piece, 0.0)
        whole = whole + piece
    outs[0][...] = outside
    if not last:
        outs[1][...] = whole.astype(outs[1].dtype)


def order(radix, reverse):
    return [1, 2, 3] if radix == 4 else list(range(radix - 1, 0, -1))


def outside_sum(total, reverse, cover):
    count, stride, group, outside = lax.axis_size("seq"), 1, total, []
    chain = radices(count)
    for at, radix in enumerate(chain):
        steps = order(radix, reverse)
        came = []
        for step in steps:
            pairs = [(s, s + (partner(s // stride % radix, step, radix) - s // stride % radix) * stride)
                     for s in range(count)]
            came.append(lax.ppermute(group, "seq", pairs))
        if at == 0:
            came, cover = lax.optimization_barrier((came, cover))
        last = at + 1 == len(chain)
        kernel = functools.partial(combine_kernel, steps, radix, stride, reverse, at == 0, last)
        sums = [((total.shape, F32), VMEM)] + ([] if last else [((total.shape, total.dtype), VMEM)])
        out = call(kernel, [(a, VMEM) for a in (group, *came, *outside)], sums, COVER)
        outside, group = out[:1], out[-1]
        stride *= radix
    return outside[0], cover


def shards(queries, key_rows, values, cotangent, out_gain, counts):
    rows, width = queries.shape
    unit = 2 * LIVE * SPAN * DH * DH
    buffer = ((rows, DH), BF16), VMEM
    half = ((LIVE * SPAN, DH), BF16), VMEM
    plane = ((LIVE * SPAN, DH), F32), VMEM
    states = ((LIVE, DH, DH), F32), VMEM
    prefixes = ((LIVE, DH, DH), BF16), VMEM
    total = ((DH, DH), BF16), VMEM
    square = ((LIVE, SPAN, SPAN), BF16), VMEM
    result = ((rows, width), BF16), HBM
    count = [(counts, SMEM)]

    def vmem(*arrays):
        return [(a, VMEM) for a in arrays]

    def sems(n):
        return pltpu.SemaphoreType.DMA((n,))

    def swap(array):
        return lax.ppermute(array, "loader", SWAP)

    pair = ((2, rows, DH), BF16), VMEM
    beside, = call(give_kernel, [(key_rows, HBM), (values, HBM)], [pair], 0, [sems(2)])
    other = swap(beside)
    loaded = call(
        load_kernel, count + [(a, HBM) for a in (key_rows, values, queries, cotangent, out_gain.reshape(1, width))],
        [buffer] * 4 + [pair, (((1, width), F32), VMEM)], 0, [sems(7)])
    other, (k_own, v_own, q_own, cot_own, give, gain) = lax.optimization_barrier((other, loaded))
    own, k, v, run = call(
        state_kernel, count + vmem(k_own, v_own, other), [total, half, half, states], unit)
    cover = call(
        score_kernel, count + vmem(q_own, cot_own, swap(give), k, v), [half, half, plane, square], 6 * unit)
    outside, (q, cot, part, turned) = outside_sum(own, False, cover)
    grad, prefix, back, own_back = call(
        norm_kernel, vmem(q, cot, gain, part, run, outside),
        [half, prefixes, states, total], 2 * unit)
    staged = [pltpu.VMEM((LIVE * SPAN, DH), kind) for kind in (BF16, F32, F32)]
    gq_own, parts, other = call(
        pull_kernel, count + vmem(q, k, v, grad, turned, prefix, back),
        [buffer, (((2, rows, DH), F32), VMEM), (((3, rows, DH), BF16), VMEM)], 13 * unit, staged)
    came = swap(other)
    outside, (gq_own, parts) = outside_sum(own_back, True, (gq_own, parts))
    return tuple(call(
        final_kernel, count + vmem(gq_own, parts, k_own, v_own, outside, came, beside, swap(outside)),
        [result] * 3, 4 * unit, [pltpu.VMEM((2, rows, DH), BF16)] * 2 + [pltpu.SemaphoreType.DMA((3, 2))]))


def solution(mesh):
    rows = P(("groups", "seq", "loader"), "head")
    return jax.shard_map(
        shards,
        mesh=mesh,
        in_specs=(rows, rows, rows, rows, P("head"), P(("groups", "seq", "loader"))),
        out_specs=(rows, rows, rows),
        check_vma=False,
    )
```

```python
import functools
import math

import jax
import jax.numpy as jnp
from jax import lax
from jax.experimental import pallas as pl
from jax.experimental.pallas import tpu as pltpu
from jax.sharding import PartitionSpec as P

DH = 128
SPAN = 256
LIVE = 6
EPSILON = 1e-06
COVER = 10**10
F32 = jnp.float32
BF16 = jnp.bfloat16
VMEM = pl.BlockSpec(memory_space=pltpu.VMEM)
SMEM = pl.BlockSpec(memory_space=pltpu.SMEM)
HBM = pl.BlockSpec(memory_space=pltpu.HBM)
SWAP = [(0, 1), (1, 0)]


def nn(a, b):
    return lax.dot_general(a, b, (((1,), (0,)), ((), ())), preferred_element_type=F32)


def nt(a, b):
    return lax.dot_general(a, b, (((1,), (1,)), ((), ())), preferred_element_type=F32)


def tn(a, b):
    return lax.dot_general(a, b, (((0,), (0,)), ((), ())), preferred_element_type=F32)


def rows_of(block):
    if isinstance(block, int):
        return slice(block * SPAN, (block + 1) * SPAN)
    return pl.ds(pl.multiple_of(block * SPAN, SPAN), SPAN)


def columns_of(core):
    return pl.ds(pl.multiple_of(core * DH, DH), DH)


def fetch(pairs, sems):
    copies = [pltpu.make_async_copy(source, target, sems.at[at]) for at, (source, target) in enumerate(pairs)]
    for copy in copies:
        copy.start()
    return copies


def wait(copies):
    for copy in copies:
        copy.wait()


def core_and_counts(count_ref):
    core, own = lax.axis_index("loader"), count_ref[0]
    return core, jnp.where(core == 0, own, LIVE - own), own


def live_block(own_ref, other_ref, at, core, count):
    late = (at >= count).astype(jnp.int32)
    r = rows_of(at - late * count)
    return jnp.where(late == core, own_ref[r, :], other_ref[r, :])


def give_kernel(k_hbm, v_hbm, give_ref, sems):
    other = columns_of(1 - lax.axis_index("loader"))
    wait(fetch([(source.at[:, other], give_ref.at[at]) for at, source in enumerate((k_hbm, v_hbm))], sems))


def load_kernel(count_ref, k_hbm, v_hbm, q_hbm, cot_hbm, gain_hbm,
                k_ref, v_ref, q_ref, cot_ref, give_ref, gain_ref, sems):
    del count_ref
    core = lax.axis_index("loader")
    own, other = columns_of(core), columns_of(1 - core)
    wait(fetch(((k_hbm.at[:, own], k_ref), (v_hbm.at[:, own], v_ref), (q_hbm.at[:, own], q_ref),
                (cot_hbm.at[:, own], cot_ref), (q_hbm.at[:, other], give_ref.at[0]),
                (cot_hbm.at[:, other], give_ref.at[1]), (gain_hbm, gain_ref)), sems))


def state_kernel(count_ref, k_own_ref, v_own_ref, other_ref, total_ref, k_ref, v_ref, run_ref):
    core, count, _ = core_and_counts(count_ref)
    running = jnp.zeros((DH, DH), F32)
    for at in range(LIVE):
        r = rows_of(at)
        k = live_block(k_own_ref, other_ref.at[0], at, core, count)
        v = live_block(v_own_ref, other_ref.at[1], at, core, count)
        k_ref[r, :], v_ref[r, :] = k, v
        run_ref[at] = running
        running = running + tn(k, v)
    total_ref[...] = running.astype(total_ref.dtype)


def score_kernel(count_ref, q_own_ref, cot_own_ref, other_ref, k_ref, v_ref,
                 q_ref, cot_ref, part_ref, turned_ref):
    core, count, _ = core_and_counts(count_ref)
    t = lax.broadcasted_iota(jnp.int32, (SPAN, SPAN), 0)
    s = lax.broadcasted_iota(jnp.int32, (SPAN, SPAN), 1)
    for at in range(LIVE):
        r = rows_of(at)
        q = live_block(q_own_ref, other_ref.at[0], at, core, count)
        q_ref[r, :] = q
        cot_ref[r, :] = live_block(cot_own_ref, other_ref.at[1], at, core, count)
        k = k_ref[r, :]
        scored = jnp.where(t >= s, nt(q, k), 0.0).astype(BF16)
        part_ref[r, :] = nn(scored, v_ref[r, :])
        turned_ref[at] = jnp.where(t <= s, nt(k, q), 0.0).astype(BF16)


def norm_kernel(q_ref, cot_ref, gain_ref, part_ref, run_ref, outside_ref,
                grad_ref, prefix_ref, back_ref, total_ref):
    outside = outside_ref[...]
    gain = gain_ref[:, columns_of(lax.axis_index("loader"))]
    running = jnp.zeros((DH, DH), F32)
    for at in reversed(range(LIVE)):
        r = rows_of(at)
        prefix = (run_ref[at] + outside).astype(BF16)
        prefix_ref[at] = prefix
        q = q_ref[r, :]
        raw = part_ref[r, :] + nn(q, prefix)
        inverse = lax.rsqrt(jnp.mean(raw * raw, axis=-1, keepdims=True) + EPSILON)
        weighted = gain * cot_ref[r, :].astype(F32)
        pulled = jnp.mean(weighted * raw, axis=-1, keepdims=True)
        grad = (inverse * weighted - raw * (inverse * inverse * inverse * pulled)).astype(BF16)
        grad_ref[r, :] = grad
        back_ref[at] = running
        running = running + tn(q, grad)
    total_ref[...] = running.astype(total_ref.dtype)


def spread(live_ref, own_ref, other_ref, core, count, own):
    for b in range(own_ref.shape[0] // SPAN):
        for target, shift, limit in (
                (own_ref, jnp.where(core == 0, 0, count), own),
                (other_ref, jnp.where(core == 0, count, 0), LIVE - own)):
            block = live_ref[rows_of(jnp.minimum(b + shift, LIVE - 1)), :]
            target[rows_of(b), :] = jnp.where(b < limit, block, jnp.zeros_like(block))


def pull_kernel(count_ref, q_ref, k_ref, v_ref, grad_ref, turned_ref, prefix_ref,
                gq_own_ref, gq_other_ref, gk_ref, gv_ref, gq_ref):
    t = lax.broadcasted_iota(jnp.int32, (SPAN, SPAN), 0)
    s = lax.broadcasted_iota(jnp.int32, (SPAN, SPAN), 1)
    for at in range(LIVE):
        r = rows_of(at)
        v, grad = v_ref[r, :], grad_ref[r, :]
        pull = jnp.where(t >= s, nt(grad, v), 0.0).astype(BF16)
        gq_ref[r, :] = (nn(pull, k_ref[r, :]) + nt(grad, prefix_ref[at])).astype(BF16)
        turned = jnp.where(t <= s, nt(v, grad), 0.0).astype(BF16)
        gk_ref[r, :] = nn(turned, q_ref[r, :])
        gv_ref[r, :] = nn(turned_ref[at], grad)
    spread(gq_ref, gq_own_ref, gq_other_ref, *core_and_counts(count_ref))


def suffix_kernel(count_ref, k_ref, v_ref, gk_part_ref, gv_part_ref, back_ref, outside_ref,
                  gk_own_ref, gv_own_ref, other_ref, gk_ref, gv_ref):
    outside = outside_ref[...]
    for at in range(LIVE):
        r = rows_of(at)
        suffix = (back_ref[at] + outside).astype(BF16)
        gk_ref[r, :] = (gk_part_ref[r, :] + nt(v_ref[r, :], suffix)).astype(BF16)
        gv_ref[r, :] = (gv_part_ref[r, :] + nn(k_ref[r, :], suffix)).astype(BF16)
    where = core_and_counts(count_ref)
    spread(gk_ref, gk_own_ref, other_ref.at[0], *where)
    spread(gv_ref, gv_own_ref, other_ref.at[1], *where)


def own_kernel(gq_own_ref, gk_own_ref, gv_own_ref, gq_hbm, gk_hbm, gv_hbm, sems):
    c = columns_of(lax.axis_index("loader"))
    wait(fetch(((gq_own_ref, gq_hbm.at[:, c]), (gk_own_ref, gk_hbm.at[:, c]), (gv_own_ref, gv_hbm.at[:, c])), sems))


def came_kernel(gq_ref, came_ref, gq_in_hbm, gk_in_hbm, gv_in_hbm, gq_hbm, gk_hbm, gv_hbm, sems):
    del gq_in_hbm, gk_in_hbm, gv_in_hbm
    c = columns_of(1 - lax.axis_index("loader"))
    wait(fetch(((gq_ref, gq_hbm.at[:, c]), (came_ref.at[0], gk_hbm.at[:, c]), (came_ref.at[1], gv_hbm.at[:, c])), sems))


def call(kernel, ins, outs, flops, scratch=(), aliases={}):
    size = sum(a.size * a.dtype.itemsize for a, _ in ins)
    size += sum(math.prod(shape) * jnp.dtype(kind).itemsize for (shape, kind), _ in outs)
    return pl.pallas_call(
        kernel,
        out_shape=[pltpu.VMEM(*a) if space is VMEM else pltpu.HBM(*a) for a, space in outs],
        in_specs=[space for _, space in ins],
        out_specs=[space for _, space in outs],
        scratch_shapes=scratch,
        input_output_aliases=aliases,
        cost_estimate=pl.CostEstimate(flops=flops, bytes_accessed=size, transcendentals=0),
        compiler_params=pltpu.CompilerParams(vmem_limit_bytes=16 * 2**20),
    )(*[a if space is SMEM else pltpu.with_memory_space_constraint(a, space.memory_space) for a, space in ins])


def radices(count):
    found = []
    for radix in (4, 2):
        while count % radix == 0:
            found.append(radix)
            count //= radix
    return found + [count] if count > 1 else found


def partner(digit, step, radix):
    return digit ^ step if radix in (2, 4) else (digit + step) % radix


def combine_kernel(steps, radix, stride, reverse, first, last, *refs):
    group_ref, came, outs = refs[0], refs[1:1 + len(steps)], refs[1 + len(steps) + (not first):]
    digit = lax.rem(lax.div(lax.axis_index("seq"), stride), radix)
    outside = jnp.zeros(outs[0].shape, F32) if first else refs[1 + len(steps)][...]
    whole = group_ref[...].astype(F32)
    for step, piece_ref in zip(steps, came):
        source = partner(digit, step if radix in (2, 4) else radix - step, radix)
        use = source > digit if reverse else source < digit
        piece = piece_ref[...].astype(F32)
        outside = outside + jnp.where(use, piece, 0.0)
        whole = whole + piece
    outs[0][...] = outside
    if not last:
        outs[1][...] = whole.astype(outs[1].dtype)


def order(radix, reverse):
    return [3, 2, 1] if radix == 4 else list(range(radix - 1, 0, -1))


def outside_sum(total, reverse, cover):
    count, stride, group, outside = lax.axis_size("seq"), 1, total, []
    chain = radices(count)
    for at, radix in enumerate(chain):
        steps = order(radix, reverse)
        came = []
        for step in steps:
            pairs = [(s, s + (partner(s // stride % radix, step, radix) - s // stride % radix) * stride)
                     for s in range(count)]
            came.append(lax.ppermute(group, "seq", pairs))
        if at == 0:
            came, cover = lax.optimization_barrier((came, cover))
        last = at + 1 == len(chain)
        kernel = functools.partial(combine_kernel, steps, radix, stride, reverse, at == 0, last)
        sums = [((total.shape, F32), VMEM)] + ([] if last else [((total.shape, total.dtype), VMEM)])
        out = call(kernel, [(a, VMEM) for a in (group, *came, *outside)], sums, COVER)
        outside, group = out[:1], out[-1]
        stride *= radix
    return outside[0], cover


def shards(queries, key_rows, values, cotangent, out_gain, counts):
    rows, width = queries.shape
    unit = 2 * LIVE * SPAN * DH * DH
    buffer = ((rows, DH), BF16), VMEM
    half = ((LIVE * SPAN, DH), BF16), VMEM
    plane = ((LIVE * SPAN, DH), F32), VMEM
    states = ((LIVE, DH, DH), F32), VMEM
    prefixes = ((LIVE, DH, DH), BF16), VMEM
    total = ((DH, DH), BF16), VMEM
    square = ((LIVE, SPAN, SPAN), BF16), VMEM
    result = ((rows, width), BF16), HBM
    staged = pltpu.VMEM((LIVE * SPAN, DH), BF16)
    count = [(counts, SMEM)]

    def vmem(*arrays):
        return [(a, VMEM) for a in arrays]

    def sems(n):
        return pltpu.SemaphoreType.DMA((n,))

    def swap(array):
        return lax.ppermute(array, "loader", SWAP)

    pair = ((2, rows, DH), BF16), VMEM
    give, = call(give_kernel, [(key_rows, HBM), (values, HBM)], [pair], 0, [sems(2)])
    other = swap(give)
    loaded = call(
        load_kernel, count + [(a, HBM) for a in (key_rows, values, queries, cotangent, out_gain.reshape(1, width))],
        [buffer] * 4 + [pair, (((1, width), F32), VMEM)], 0, [sems(7)])
    other, (k_own, v_own, q_own, cot_own, give, gain) = lax.optimization_barrier((other, loaded))
    own, k, v, run = call(
        state_kernel, count + vmem(k_own, v_own, other), [total, half, half, states], unit)
    cover = call(
        score_kernel, count + vmem(q_own, cot_own, swap(give), k, v), [half, half, plane, square], 6 * unit)
    outside, (q, cot, part, turned) = outside_sum(own, False, cover)
    grad, prefix, back, own_back = call(
        norm_kernel, vmem(q, cot, gain, part, run, outside),
        [half, prefixes, states, total], 2 * unit)
    gq_own, gq_other, gk_part, gv_part = call(
        pull_kernel, count + vmem(q, k, v, grad, turned, prefix), [buffer, buffer, plane, plane], 11 * unit, [staged])
    gq_came = swap(gq_other)
    outside, (gq_own, gk_part, gv_part) = outside_sum(own_back, True, (gq_own, gk_part, gv_part))
    gk_own, gv_own, other = call(
        suffix_kernel, count + vmem(k, v, gk_part, gv_part, back, outside),
        [buffer, buffer, pair], 2 * unit, [staged, staged])
    came = swap(other)
    grads = call(own_kernel, vmem(gq_own, gk_own, gv_own), [result] * 3, 0, [sems(3)])
    came, grads = lax.optimization_barrier((came, grads))
    return tuple(call(
        came_kernel, vmem(gq_came, came) + [(grad, HBM) for grad in grads], [result] * 3, 0, [sems(3)],
        {2: 0, 3: 1, 4: 2}))


def solution(mesh):
    rows = P(("groups", "seq", "loader"), "head")
    return jax.shard_map(
        shards,
        mesh=mesh,
        in_specs=(rows, rows, rows, rows, P("head"), P(("groups", "seq", "loader"))),
        out_specs=(rows, rows, rows),
        check_vma=False,
    )
```

```python
import functools
import math

import jax
import jax.numpy as jnp
from jax import lax
from jax.experimental import pallas as pl
from jax.experimental.pallas import tpu as pltpu
from jax.sharding import PartitionSpec as P

DH = 128
SPAN = 256
LIVE = 6
EPSILON = 1e-06
F32 = jnp.float32
BF16 = jnp.bfloat16
VMEM = pl.BlockSpec(memory_space=pltpu.VMEM)
SMEM = pl.BlockSpec(memory_space=pltpu.SMEM)
HBM = pl.BlockSpec(memory_space=pltpu.HBM)
SWAP = [(0, 1), (1, 0)]


def nn(a, b):
    return lax.dot_general(a, b, (((1,), (0,)), ((), ())), preferred_element_type=F32)


def nt(a, b):
    return lax.dot_general(a, b, (((1,), (1,)), ((), ())), preferred_element_type=F32)


def tn(a, b):
    return lax.dot_general(a, b, (((0,), (0,)), ((), ())), preferred_element_type=F32)


def rows_of(block):
    if isinstance(block, int):
        return slice(block * SPAN, (block + 1) * SPAN)
    return pl.ds(pl.multiple_of(block * SPAN, SPAN), SPAN)


def columns_of(core):
    return pl.ds(pl.multiple_of(core * DH, DH), DH)


def fetch(pairs, sems):
    copies = [pltpu.make_async_copy(source, target, sems.at[at]) for at, (source, target) in enumerate(pairs)]
    for copy in copies:
        copy.start()
    return copies


def wait(copies):
    for copy in copies:
        copy.wait()


def core_and_counts(count_ref):
    core, own = lax.axis_index("loader"), count_ref[0]
    return core, jnp.where(core == 0, own, LIVE - own), own


def live_block(own_ref, other_ref, at, core, count):
    late = (at >= count).astype(jnp.int32)
    r = rows_of(at - late * count)
    return jnp.where(late == core, own_ref[r, :], other_ref[r, :])


def give_kernel(k_hbm, v_hbm, give_ref, sems):
    other = columns_of(1 - lax.axis_index("loader"))
    wait(fetch([(source.at[:, other], give_ref.at[at]) for at, source in enumerate((k_hbm, v_hbm))], sems))


def load_kernel(count_ref, k_hbm, v_hbm, q_hbm, cot_hbm, gain_hbm,
                k_ref, v_ref, q_ref, cot_ref, give_ref, gain_ref, sems):
    del count_ref
    core = lax.axis_index("loader")
    own, other = columns_of(core), columns_of(1 - core)
    wait(fetch(((k_hbm.at[:, own], k_ref), (v_hbm.at[:, own], v_ref), (q_hbm.at[:, own], q_ref),
                (cot_hbm.at[:, own], cot_ref), (q_hbm.at[:, other], give_ref.at[0]),
                (cot_hbm.at[:, other], give_ref.at[1]), (gain_hbm, gain_ref)), sems))


def state_kernel(count_ref, k_own_ref, v_own_ref, other_ref, total_ref, k_ref, v_ref, run_ref):
    core, count, _ = core_and_counts(count_ref)
    running = jnp.zeros((DH, DH), F32)
    for at in range(LIVE):
        r = rows_of(at)
        k = live_block(k_own_ref, other_ref.at[0], at, core, count)
        v = live_block(v_own_ref, other_ref.at[1], at, core, count)
        k_ref[r, :], v_ref[r, :] = k, v
        run_ref[at] = running
        running = running + tn(k, v)
    total_ref[...] = running.astype(total_ref.dtype)


def score_kernel(count_ref, q_own_ref, cot_own_ref, other_ref, k_ref, v_ref,
                 q_ref, cot_ref, part_ref, turned_ref):
    core, count, _ = core_and_counts(count_ref)
    t = lax.broadcasted_iota(jnp.int32, (SPAN, SPAN), 0)
    s = lax.broadcasted_iota(jnp.int32, (SPAN, SPAN), 1)
    for at in range(LIVE):
        r = rows_of(at)
        q = live_block(q_own_ref, other_ref.at[0], at, core, count)
        q_ref[r, :] = q
        cot_ref[r, :] = live_block(cot_own_ref, other_ref.at[1], at, core, count)
        k = k_ref[r, :]
        scored = jnp.where(t >= s, nt(q, k), 0.0).astype(BF16)
        part_ref[r, :] = nn(scored, v_ref[r, :])
        turned_ref[at] = jnp.where(t <= s, nt(k, q), 0.0).astype(BF16)


def norm_kernel(q_ref, cot_ref, gain_ref, part_ref, run_ref, outside_ref,
                grad_ref, prefix_ref, back_ref, total_ref):
    outside = outside_ref[...]
    gain = gain_ref[:, columns_of(lax.axis_index("loader"))]
    running = jnp.zeros((DH, DH), F32)
    for at in reversed(range(LIVE)):
        r = rows_of(at)
        prefix = (run_ref[at] + outside).astype(BF16)
        prefix_ref[at] = prefix
        q = q_ref[r, :]
        raw = part_ref[r, :] + nn(q, prefix)
        inverse = lax.rsqrt(jnp.mean(raw * raw, axis=-1, keepdims=True) + EPSILON)
        weighted = gain * cot_ref[r, :].astype(F32)
        pulled = jnp.mean(weighted * raw, axis=-1, keepdims=True)
        grad = (inverse * (weighted - raw * (inverse * inverse * pulled))).astype(BF16)
        grad_ref[r, :] = grad
        back_ref[at] = running
        running = running + tn(q, grad)
    total_ref[...] = running.astype(total_ref.dtype)


def spread(live_ref, own_ref, other_ref, core, count, own):
    for b in range(own_ref.shape[0] // SPAN):
        for target, shift, limit in (
                (own_ref, jnp.where(core == 0, 0, count), own),
                (other_ref, jnp.where(core == 0, count, 0), LIVE - own)):
            block = live_ref[rows_of(jnp.minimum(b + shift, LIVE - 1)), :]
            target[rows_of(b), :] = jnp.where(b < limit, block, jnp.zeros_like(block))


def pull_kernel(count_ref, q_ref, k_ref, v_ref, grad_ref, turned_ref, prefix_ref,
                gq_own_ref, other_ref, gk_ref, gv_ref, gq_ref):
    t = lax.broadcasted_iota(jnp.int32, (SPAN, SPAN), 0)
    s = lax.broadcasted_iota(jnp.int32, (SPAN, SPAN), 1)
    for at in range(LIVE):
        r = rows_of(at)
        v, grad = v_ref[r, :], grad_ref[r, :]
        pull = jnp.where(t >= s, nt(grad, v), 0.0).astype(BF16)
        gq_ref[r, :] = (nn(pull, k_ref[r, :]) + nt(grad, prefix_ref[at])).astype(BF16)
        turned = jnp.where(t <= s, nt(v, grad), 0.0).astype(BF16)
        gk_ref[r, :] = nn(turned, q_ref[r, :])
        gv_ref[r, :] = nn(turned_ref[at], grad)
    spread(gq_ref, gq_own_ref, other_ref.at[0], *core_and_counts(count_ref))


def suffix_kernel(count_ref, k_ref, v_ref, gk_part_ref, gv_part_ref, back_ref, outside_ref, begun_ref,
                  gk_own_ref, gv_own_ref, other_ref, gk_ref, gv_ref):
    del begun_ref
    outside = outside_ref[...]
    for at in range(LIVE):
        r = rows_of(at)
        suffix = (back_ref[at] + outside).astype(BF16)
        gk_ref[r, :] = (gk_part_ref[r, :] + nt(v_ref[r, :], suffix)).astype(BF16)
        gv_ref[r, :] = (gv_part_ref[r, :] + nn(k_ref[r, :], suffix)).astype(BF16)
    where = core_and_counts(count_ref)
    spread(gk_ref, gk_own_ref, other_ref.at[1], *where)
    spread(gv_ref, gv_own_ref, other_ref.at[2], *where)


def own_kernel(gq_own_ref, gk_own_ref, gv_own_ref, gq_hbm, gk_hbm, gv_hbm, sems):
    c = columns_of(lax.axis_index("loader"))
    wait(fetch(((gq_own_ref, gq_hbm.at[:, c]), (gk_own_ref, gk_hbm.at[:, c]), (gv_own_ref, gv_hbm.at[:, c])), sems))


def came_kernel(came_ref, gq_in_hbm, gk_in_hbm, gv_in_hbm, gq_hbm, gk_hbm, gv_hbm, sems):
    del gq_in_hbm, gk_in_hbm, gv_in_hbm
    c = columns_of(1 - lax.axis_index("loader"))
    wait(fetch([(came_ref.at[at], target.at[:, c]) for at, target in enumerate((gq_hbm, gk_hbm, gv_hbm))], sems))


def call(kernel, ins, outs, flops, scratch=(), aliases={}):
    size = sum(a.size * a.dtype.itemsize for a, _ in ins)
    size += sum(math.prod(shape) * jnp.dtype(kind).itemsize for (shape, kind), _ in outs)
    return pl.pallas_call(
        kernel,
        out_shape=[pltpu.VMEM(*a) if space is VMEM else pltpu.HBM(*a) for a, space in outs],
        in_specs=[space for _, space in ins],
        out_specs=[space for _, space in outs],
        scratch_shapes=scratch,
        input_output_aliases=aliases,
        cost_estimate=pl.CostEstimate(flops=flops, bytes_accessed=size, transcendentals=0),
        compiler_params=pltpu.CompilerParams(vmem_limit_bytes=16 * 2**20),
    )(*[a if space is SMEM else pltpu.with_memory_space_constraint(a, space.memory_space) for a, space in ins])


def radices(count):
    found = []
    for radix in (4, 2):
        while count % radix == 0:
            found.append(radix)
            count //= radix
    return found + [count] if count > 1 else found


def partner(digit, step, radix):
    return digit ^ step if radix in (2, 4) else (digit + step) % radix


def combine_kernel(steps, radix, stride, reverse, first, last, *refs):
    group_ref, came, outs = refs[0], refs[1:1 + len(steps)], refs[1 + len(steps) + (not first):]
    digit = lax.rem(lax.div(lax.axis_index("seq"), stride), radix)
    outside = jnp.zeros(outs[0].shape, F32) if first else refs[1 + len(steps)][...]
    whole = group_ref[...].astype(F32)
    for step, piece_ref in zip(steps, came):
        source = partner(digit, step if radix in (2, 4) else radix - step, radix)
        use = source > digit if reverse else source < digit
        piece = piece_ref[...].astype(F32)
        outside = outside + jnp.where(use, piece, 0.0)
        whole = whole + piece
    outs[0][...] = outside
    if not last:
        outs[1][...] = whole.astype(outs[1].dtype)


def order(radix, reverse):
    return [3, 2, 1] if radix == 4 else list(range(radix - 1, 0, -1))


def outside_sum(total, reverse, cover):
    count, stride, group, outside = lax.axis_size("seq"), 1, total, []
    chain = radices(count)
    for at, radix in enumerate(chain):
        steps = order(radix, reverse)
        came = []
        for step in steps:
            pairs = [(s, s + (partner(s // stride % radix, step, radix) - s // stride % radix) * stride)
                     for s in range(count)]
            came.append(lax.ppermute(group, "seq", pairs))
        if at == 0:
            came, cover = lax.optimization_barrier((came, cover))
        last = at + 1 == len(chain)
        kernel = functools.partial(combine_kernel, steps, radix, stride, reverse, at == 0, last)
        sums = [((total.shape, F32), VMEM)] + ([] if last else [((total.shape, total.dtype), VMEM)])
        out = call(kernel, [(a, VMEM) for a in (group, *came, *outside)], sums, total.size)
        outside, group = out[:1], out[-1]
        stride *= radix
    return outside[0], cover


def shards(queries, key_rows, values, cotangent, out_gain, counts):
    rows, width = queries.shape
    unit = 2 * LIVE * SPAN * DH * DH
    buffer = ((rows, DH), BF16), VMEM
    half = ((LIVE * SPAN, DH), BF16), VMEM
    plane = ((LIVE * SPAN, DH), F32), VMEM
    states = ((LIVE, DH, DH), F32), VMEM
    prefixes = ((LIVE, DH, DH), BF16), VMEM
    total = ((DH, DH), BF16), VMEM
    square = ((LIVE, SPAN, SPAN), BF16), VMEM
    result = ((rows, width), BF16), HBM
    staged = pltpu.VMEM((LIVE * SPAN, DH), BF16)
    count = [(counts, SMEM)]

    def vmem(*arrays):
        return [(a, VMEM) for a in arrays]

    def sems(n):
        return pltpu.SemaphoreType.DMA((n,))

    def swap(array):
        return lax.ppermute(array, "loader", SWAP)

    pair = ((2, rows, DH), BF16), VMEM
    give, = call(give_kernel, [(key_rows, HBM), (values, HBM)], [pair], 0, [sems(2)])
    other = swap(give)
    loaded = call(
        load_kernel, count + [(a, HBM) for a in (key_rows, values, queries, cotangent, out_gain.reshape(1, width))],
        [buffer] * 4 + [pair, (((1, width), F32), VMEM)], 0, [sems(7)])
    other, (k_own, v_own, q_own, cot_own, give, gain) = lax.optimization_barrier((other, loaded))
    own, k, v, run = call(
        state_kernel, count + vmem(k_own, v_own, other), [total, half, half, states], unit)
    cover = call(
        score_kernel, count + vmem(q_own, cot_own, swap(give), k, v), [half, half, plane, square], 6 * unit)
    outside, (q, cot, part, turned) = outside_sum(own, False, cover)
    grad, prefix, back, own_back = call(
        norm_kernel, vmem(q, cot, gain, part, run, outside),
        [half, prefixes, states, total], 2 * unit)
    three = ((3, rows, DH), BF16), VMEM
    cover = call(
        pull_kernel, count + vmem(q, k, v, grad, turned, prefix), [buffer, three, plane, plane], 11 * unit, [staged])
    outside, (gq_own, other, gk_part, gv_part) = outside_sum(own_back, True, cover)
    gk_own, gv_own, other = call(
        suffix_kernel, count + vmem(k, v, gk_part, gv_part, back, outside, other),
        [buffer, buffer, three], 2 * unit, [staged, staged], {7: 2})
    came = swap(other)
    grads = call(own_kernel, vmem(gq_own, gk_own, gv_own), [result] * 3, 0, [sems(3)])
    came, grads = lax.optimization_barrier((came, grads))
    return tuple(call(
        came_kernel, vmem(came) + [(grad, HBM) for grad in grads], [result] * 3, 0, [sems(3)], {1: 0, 2: 1, 3: 2}))


def solution(mesh):
    rows = P(("groups", "seq", "loader"), "head")
    return jax.shard_map(
        shards,
        mesh=mesh,
        in_specs=(rows, rows, rows, rows, P("head"), P(("groups", "seq", "loader"))),
        out_specs=(rows, rows, rows),
        check_vma=False,
    )
```
